512 devices in a mesh: elem: 32 (over z, y_lo), mode: 16 (over x, y_hi, core).
Axes of the slice: x: 4, y: 8 (y_hi: 2, y_lo: 4; y = y_hi * 4 + y_lo), z: 8, core: 2. Of those that a mesh axis runs over, the one named last changes fastest.
Arguments:
- modal_history: float32 [4096, 512], P('elem', 'mode'), may hold values from -6 to 6
- stress_modes: float32 [512, 6144], P('mode', 'elem'), may hold values from -0.5 to 0.5
Outputs:
- stress_spectrum: float32 [6144, 2, 2048], P(('elem', 'mode'))
The draws below stay inside these ranges and needn't reach their ends.
All inputs are finite; a program needn't handle non-finite values.
Results may differ from the reference program's by a relative error of at most 0.00007.
Values sent between devices are 32-bit elements; how exact they have to be, the bound alone decides.
No kernel may reach another device: no remote copies, remote signals or barrier semaphores. Data moves between devices by JAX's collectives and lax.ppermute only.
A program may use at most 64 MiB of HBM per device.

```python
import jax
import jax.numpy as jnp
from jax import lax

M = 512
NT = 4096
C = 6
E = 1024


def raised(entries, own_key, source, target, blocks, factor):
    owner, partner = [(jnp.arange(entries.shape[dim]) // (entries.shape[dim] // blocks)).reshape([-1 if axis == dim else 1 for axis in range(entries.ndim)]) for dim in (source, target)]
    chosen = jax.random.permutation(own_key, blocks)[partner]
    strong = (owner == chosen) | (owner == (partner + blocks // 2) % blocks)
    return jnp.where(strong, factor * entries, entries)


def block_levels(rng, extent, cuts, low, top_value):
    factor_of = 1.0
    for axis_at, shards_of in cuts:
        draws = jax.random.uniform(jax.random.fold_in(jax.random.fold_in(rng, 6), axis_at), (shards_of,), jnp.float32, low / len(cuts), top_value / len(cuts))
        factor_of = factor_of * jnp.repeat(jnp.exp(draws), extent[axis_at] // shards_of).reshape((-1,) + (1,) * (len(extent) - 1 - axis_at))
    return factor_of


def gaussian(stream_key, shape, spread, most, pieces=(), dtype=jnp.bfloat16):
    level = block_levels(stream_key, shape, pieces, -0.22, 0.18) if pieces else 1.0
    drawn = jax.random.normal(stream_key, shape, jnp.float32) * spread * level
    return jnp.minimum(jnp.maximum(drawn, -most), most).astype(dtype)


def gaussian_with(own_key, dims, deviation, bound, cuts, heavy, held_as=jnp.bfloat16):
    entries = deviation * jax.random.normal(own_key, dims, jnp.float32)
    if cuts:
        entries = entries * block_levels(own_key, dims, cuts, -0.22, 0.18)
    return jnp.clip(raised(entries, jax.random.fold_in(own_key, 3), *heavy), -bound, bound).astype(held_as)


def setup_inputs(seed: int = 0) -> dict:
    key_of = jax.random.split(jax.random.key(seed), 3)
    return {
        "modal_history": gaussian(key_of[0], (NT, M), 1.0, 6.0, ((0, 32), (1, 16)), jnp.float32),
        "stress_modes": gaussian_with(key_of[1], (M, E * C), M ** -0.5, 0.5, ((0, 16), (1, 32)), (0, 1, 32, 2.75), jnp.float32),
    }


def reference(modal_history, stress_modes):
    stress = jnp.dot(stress_modes.T, modal_history.T, precision=lax.Precision.HIGHEST, preferred_element_type=jnp.float32)
    spectrum = jnp.fft.rfft(stress, axis=1, norm="ortho")[:, : NT // 2]
    return jnp.stack([jnp.real(spectrum), jnp.imag(spectrum)], axis=1).astype(jnp.float32)
```

```python
import numpy as np

import jax
import jax.numpy as jnp
from jax import lax
from jax.sharding import Mesh, PartitionSpec as P

highest = lax.Precision.HIGHEST

PARTS = ("z", "yl", "x", "yh", "c")
SIZES = (8, 4, 4, 2, 2)
ELEM = ("z", "yl")
MODE = ("x", "yh", "c")
PAIR = ("x", "c")
STEPS = 4096
SLOW, FAST = 128, 32


def tables():
    k1 = np.arange(SLOW)
    n1 = np.arange(SLOW)
    angle = 2.0 * np.pi * ((n1[:, None] * k1[None, :]) % SLOW) / SLOW
    eye = np.eye(4)
    first = np.stack([np.cos(angle), -np.sin(angle)], axis=1)
    first = np.einsum("npk,bc->nbcpk", first, eye).reshape(4 * SLOW, 4 * 2 * SLOW)
    n2 = np.arange(FAST)
    turn = 2.0 * np.pi * (n2[:, None] * k1[None, :]) / STEPS
    twist = np.stack([np.cos(turn), -np.sin(turn)])
    k2 = np.arange(FAST // 2)
    angle = 2.0 * np.pi * ((n2[:, None] * k2[None, :]) % FAST) / FAST
    real, imag = np.cos(angle) / 64.0, -np.sin(angle) / 64.0
    last = np.stack([np.stack([real, -imag]), np.stack([imag, real])])
    return [np.asarray(a, np.float32) for a in (first, twist, last)]


def spectra(gathered):
    first, twist, last = tables()
    summed = gathered[:, 0] + gathered[:, 1]
    columns = summed.shape[2]
    rows = summed.reshape(8 * columns, 4 * SLOW)
    stage = jnp.dot(rows, first, precision=highest).reshape(8, columns, 4, 2, SLOW)
    stage = stage.transpose(3, 1, 0, 2, 4).reshape(2, columns, FAST, SLOW)
    turned = jnp.stack(
        [
            stage[0] * twist[0] - stage[1] * twist[1],
            stage[0] * twist[1] + stage[1] * twist[0],
        ]
    )
    out = jnp.einsum("oink,icna->coka", last, turned, precision=highest)
    return out.reshape(columns, 2, STEPS // 2)


def per_device(modal_history, stress_modes):
    local_modes, width = stress_modes.shape
    pieces = modal_history.T.reshape(local_modes, 4, 8, 4).transpose(2, 0, 1, 3)
    pieces = pieces.reshape(8, local_modes, 16)
    sent = jnp.concatenate(
        [jnp.broadcast_to(stress_modes, (8, local_modes, width)), pieces], axis=2
    )
    got = lax.all_to_all(sent, PAIR, split_axis=0, concat_axis=0, tiled=True)
    modes = got[:, :, :width].reshape(8 * local_modes, width)
    history = got[:, :, width:].reshape(8 * local_modes, 16).T
    spread = jnp.broadcast_to(history, (32,) + history.shape)
    steps = lax.all_to_all(spread, ELEM, split_axis=0, concat_axis=0, tiled=True)
    steps = steps.reshape(32 * 16, 8 * local_modes)
    partial = jnp.einsum("mp,tm->pt", modes, steps, precision=highest)
    partial = partial.reshape(16, width // 16, 32 * 16)
    owned = lax.all_to_all(partial, MODE, split_axis=0, concat_axis=0, tiled=True)
    return spectra(owned.reshape(4, 2, 2, width // 16, 32 * 16))


def solution(mesh):
    parts = Mesh(mesh.devices.reshape(SIZES), PARTS)
    return jax.shard_map(
        per_device,
        mesh=parts,
        in_specs=(P(ELEM, MODE), P(MODE, ELEM)),
        out_specs=P(PARTS, None, None),
        check_vma=False,
    )
```

```python
import numpy as np

import jax
import jax.numpy as jnp
from jax import lax
from jax.experimental import pallas as pl
from jax.experimental.pallas import tpu as pltpu
from jax.sharding import Mesh, PartitionSpec as P

PARTS = ("z", "yl", "x", "yh", "c")
SIZES = (8, 4, 4, 2, 2)
ELEM = ("z", "yl")
MODE = ("x", "yh", "c")
BLOCKS, SHARES = 32, 16
STEPS, MODES = 4096, 512
SLOW, FAST = 256, 16
OWNED, PADDED = 12, 16
LANES = 128
f32, bf16 = jnp.float32, jnp.bfloat16
NN = (((1,), (0,)), ((), ()))
NT = (((1,), (1,)), ((), ()))


def split(x):
    high = x.astype(bf16)
    return high, (x - high.astype(f32)).astype(bf16)


def product(a, b, dims):
    (ah, al), (bh, bl) = a, b
    dot = lambda x, y: lax.dot_general(x, y, dims, preferred_element_type=f32)
    return dot(ah, bh) + (dot(ah, bl) + dot(al, bh))


def tables():
    k1 = np.arange(SLOW)
    angle = 2.0 * np.pi * ((k1[:, None] * k1[None, :]) % SLOW) / SLOW
    first = np.concatenate([np.cos(angle), -np.sin(angle)], axis=1) / np.sqrt(STEPS)
    high = first.astype(np.float32).astype(jnp.bfloat16)
    low = (first - high.astype(np.float64)).astype(jnp.bfloat16)
    turn = 2.0 * np.pi * (np.arange(FAST)[:, None] * k1[None, :]) / STEPS
    twist = np.stack([np.cos(turn), -np.sin(turn)])
    return high, low, twist.astype(np.float32)


def share():
    return lax.axis_index(MODE)


def scatter_steps(history_ref, out_ref, wide, tall):
    modes = history_ref.shape[0]
    wide[...] = jnp.zeros_like(wide)
    at = pl.multiple_of(lax.rem(share(), LANES // modes) * modes, modes)
    wide[pl.ds(at, modes), :] = history_ref[...]
    tall[...] = wide[...].T
    for n2 in range(FAST):
        out_ref[n2] = tall[pl.ds(n2, LANES // FAST, stride=FAST), :]


def join_shares(got_ref, out_ref):
    for quad in range(4):
        joined = (got_ref[4 * quad] + got_ref[4 * quad + 1]) + (
            got_ref[4 * quad + 2] + got_ref[4 * quad + 3]
        )
        lanes = pl.ds(quad * LANES, LANES)
        out_ref[:, :, lanes] = jnp.broadcast_to(joined, (BLOCKS,) + joined.shape)


def order_modes(own_ref, one_ref, two_ref, three_ref, high_ref, low_ref, whole):
    x, y, c = lax.axis_index("x"), lax.axis_index("yh"), lax.axis_index("c")
    rows = own_ref.shape[0] // 4
    for shift, ref in enumerate((own_ref, one_ref, two_ref, three_ref)):
        at_x = lax.rem(x + 4 - shift, 4)
        for part in range(4):
            at_y = lax.rem(y + part % 2, 2)
            at_c = lax.rem(c + part // 2, 2)
            at = pl.multiple_of((at_x * 4 + at_y * 2 + at_c) * rows, rows)
            whole[pl.ds(at, rows), :] = ref[pl.ds(part * rows, rows), :]
    high_ref[...], low_ref[...] = split(whole[...].T)


def contract(high_ref, low_ref, steps_ref, out_ref):
    steps = steps_ref[...].reshape(SLOW, MODES)
    stress = product((high_ref[...], low_ref[...]), split(steps), NT)
    for owner in range(SHARES):
        out_ref[owner] = stress[owner * OWNED : (owner + 1) * OWNED, :]


def plus(a, b):
    return a[0] + b[0], a[1] + b[1]


def minus(a, b):
    return a[0] - b[0], a[1] - b[1]


def by_minus_i(a):
    return a[1], -a[0]


def times(a, real, imag):
    return a[0] * real - a[1] * imag, a[0] * imag + a[1] * real


def transform(values):
    size = len(values)
    if size == 1:
        return values
    even, odd = transform(values[::2]), transform(values[1::2])
    low, high = [], []
    for k in range(size // 2):
        turned = odd[k]
        if 4 * k == size:
            turned = by_minus_i(turned)
        elif k:
            turned = times(
                turned,
                float(np.cos(2 * np.pi * k / size)),
                float(-np.sin(2 * np.pi * k / size)),
            )
        low.append(plus(even[k], turned))
        high.append(minus(even[k], turned))
    return low + high


def spectra(got_ref, high_ref, low_ref, twist_ref, out_ref, rows_high, rows_low, stage):
    for n2 in range(FAST):
        high, low = split(got_ref[n2])
        rows_high[pl.ds(n2 * PADDED, OWNED), :] = high
        rows_low[pl.ds(n2 * PADDED, OWNED), :] = low
    stage[...] = product(
        (rows_high[...], rows_low[...]), (high_ref[...], low_ref[...]), NN
    )
    tiles = STEPS // 2 // LANES
    for top in range(0, OWNED, 8):
        for left in range(0, SLOW, LANES):
            values = []
            for n2 in range(FAST):
                rows = pl.ds(n2 * PADDED + top, 8)
                value = (
                    stage[rows, pl.ds(left, LANES)],
                    stage[rows, pl.ds(SLOW + left, LANES)],
                )
                if n2:
                    lanes = pl.ds(left, LANES)
                    value = times(
                        value,
                        twist_ref[0, pl.ds(n2, 1), lanes],
                        twist_ref[1, pl.ds(n2, 1), lanes],
                    )
                values.append(value)
            valid = min(8, OWNED - top)
            for k2, value in enumerate(transform(values)[: FAST // 2]):
                tile = (k2 * SLOW + left) // LANES
                for part in range(2):
                    first = (top * tiles + tile) * 2 + part
                    to = pl.ds(first, valid, stride=2 * tiles)
                    out_ref[to, :] = value[part][:valid]


def call(kernel, shapes, *args, scratch=(), flops=0):
    whole = pl.BlockSpec(memory_space=pltpu.VMEM)
    return pl.pallas_call(
        kernel,
        out_shape=shapes,
        in_specs=[whole] * len(args),
        out_specs=jax.tree.map(lambda _: whole, shapes),
        scratch_shapes=scratch,
        compiler_params=pltpu.CompilerParams(vmem_limit_bytes=8 << 20),
        cost_estimate=pl.CostEstimate(
            flops=flops,
            transcendentals=0,
            bytes_accessed=sum(a.size * a.dtype.itemsize for a in args),
        ),
    )(*args)


def swap(x, axis):
    return lax.ppermute(x, axis, [(0, 1), (1, 0)])


def per_device(modal_history, stress_modes):
    modes, width = stress_modes.shape
    shape = jax.ShapeDtypeStruct
    vmem = pltpu.VMEM
    sent = call(
        scatter_steps,
        shape((SHARES, LANES // FAST, LANES), f32),
        modal_history.T,
        scratch=[vmem((LANES, LANES), f32)] * 2,
    )
    got = lax.all_to_all(sent, MODE, split_axis=0, concat_axis=0, tiled=True)
    pair = jnp.concatenate([stress_modes, swap(stress_modes, "yh")])
    quad = jnp.concatenate([pair, swap(pair, "c")])
    quads = [quad] + [
        lax.ppermute(quad, "x", [(i, (i + k) % 4) for i in range(4)]) for k in (1, 2, 3)
    ]
    high, low = call(
        order_modes,
        (shape((width, MODES), bf16), shape((width, MODES), bf16)),
        *quads,
        scratch=[vmem((MODES, width), f32)],
    )
    spread = call(join_shares, shape((BLOCKS, LANES // FAST, MODES), f32), got)
    steps = lax.all_to_all(spread, ELEM, split_axis=0, concat_axis=0, tiled=True)
    stress = call(contract, shape((SHARES, OWNED, SLOW), f32), high, low, steps)
    owned = lax.all_to_all(stress, MODE, split_axis=0, concat_axis=0, tiled=True)
    first_high, first_low, twist = tables()
    rows = FAST * PADDED
    out = call(
        spectra,
        shape((OWNED * STEPS // LANES, LANES), f32),
        owned,
        first_high,
        first_low,
        twist,
        scratch=[vmem((rows, SLOW), bf16)] * 2 + [vmem((rows, 2 * SLOW), f32)],
    )
    out = out.reshape(OWNED, STEPS // 2 // LANES, 2, LANES).transpose(0, 2, 1, 3)
    return out.reshape(OWNED, 2, STEPS // 2)


def solution(mesh):
    parts = Mesh(mesh.devices.reshape(SIZES), PARTS)
    return jax.shard_map(
        per_device,
        mesh=parts,
        in_specs=(P(ELEM, MODE), P(MODE, ELEM)),
        out_specs=P(PARTS, None, None),
        check_vma=False,
    )
```

```python
import numpy as np

import jax
import jax.numpy as jnp
from jax import lax
from jax.experimental import pallas as pl
from jax.experimental.pallas import tpu as pltpu
from jax.sharding import Mesh, PartitionSpec as P

PARTS = ("z", "yl", "x", "yh", "c")
SIZES = (8, 4, 4, 2, 2)
ELEM = ("z", "yl")
MODE = ("x", "yh", "c")
BLOCKS, SHARES = 32, 16
STEPS, MODES = 4096, 512
SLOW, FAST = 256, 16
OWNED, PADDED = 12, 16
LANES = 128
f32, bf16 = jnp.float32, jnp.bfloat16
NN = (((1,), (0,)), ((), ()))
NT = (((1,), (1,)), ((), ()))


def split(x):
    high = x.astype(bf16)
    return high, (x - high.astype(f32)).astype(bf16)


def product(a, b, dims):
    (ah, al), (bh, bl) = a, b
    dot = lambda x, y: lax.dot_general(x, y, dims, preferred_element_type=f32)
    return dot(ah, bh) + (dot(ah, bl) + dot(al, bh))


def tables():
    k1 = np.arange(SLOW)
    angle = 2.0 * np.pi * ((k1[:, None] * k1[None, :]) % SLOW) / SLOW
    first = np.concatenate([np.cos(angle), -np.sin(angle)], axis=1) / np.sqrt(STEPS)
    first = first.reshape(BLOCKS, 2, 4, 2 * SLOW).transpose(2, 0, 1, 3)
    first = first.reshape(SLOW, 2 * SLOW)
    high = first.astype(np.float32).astype(jnp.bfloat16)
    low = (first - high.astype(np.float64)).astype(jnp.bfloat16)
    turn = 2.0 * np.pi * (np.arange(FAST)[:, None] * k1[None, :]) / STEPS
    twist = np.stack([np.cos(turn), -np.sin(turn)])
    return high, low, twist.astype(np.float32)


def scatter_steps(history_ref, out_ref, wide, tall):
    modes = history_ref.shape[0]
    wide[...] = jnp.zeros_like(wide)
    wide[pl.ds(0, modes), :] = history_ref[...]
    tall[...] = wide[...].T
    turn = lax.rem(lax.axis_index(MODE), 4)
    for half in range(2):
        joined = None
        for quarter in range(4):
            rows = tall[pl.ds((4 * half + quarter) * FAST, FAST), :]
            rows = pltpu.roll(rows, lax.rem(quarter + turn, 4) * modes, 1)
            joined = rows if joined is None else joined + rows
        wide[pl.ds(half * FAST, FAST), :] = joined
    odd = lax.broadcasted_iota(jnp.int32, (2 * BLOCKS, LANES), 0) % 2 == 1
    for owner in range(SHARES):
        first = jnp.broadcast_to(wide[pl.ds(owner, 1), :], odd.shape)
        second = jnp.broadcast_to(wide[pl.ds(FAST + owner, 1), :], odd.shape)
        out_ref[pl.ds(owner * 2 * BLOCKS, 2 * BLOCKS), :] = jnp.where(odd, second, first)


def order_modes(own_ref, y_ref, c_ref, both_ref, high_ref, low_ref, whole):
    x, y, c = lax.axis_index("x"), lax.axis_index("yh"), lax.axis_index("c")
    rows = own_ref.shape[0] // 4
    for other, ref in enumerate((own_ref, y_ref, c_ref, both_ref)):
        at_y = lax.rem(y + other % 2, 2)
        at_c = lax.rem(c + other // 2, 2)
        for shift in range(4):
            at_x = lax.rem(x + 4 - shift, 4)
            at = pl.multiple_of((at_x * 4 + at_y * 2 + at_c) * rows, rows)
            whole[pl.ds(at, rows), :] = ref[pl.ds(shift * rows, rows), :]
    high_ref[...], low_ref[...] = split(whole[...].T)


def contract(high_ref, low_ref, got_ref, out_ref, steps_high, steps_low):
    rows = 2 * BLOCKS
    block = lax.broadcasted_iota(jnp.int32, (rows, LANES), 1) // (LANES // 4)
    for quad in range(SHARES // 4):
        shares = [got_ref[pl.ds((4 * quad + k) * rows, rows), :] for k in range(4)]
        for quarter in range(4):
            value = shares[-quarter % 4]
            for k in range(1, 4):
                value = jnp.where(block == k, shares[(k - quarter) % 4], value)
            if quarter:
                value = pltpu.roll(value, LANES - quarter * LANES // 4, 1)
            at = (pl.ds(quarter * rows, rows), pl.ds(quad * LANES, LANES))
            steps_high[at], steps_low[at] = split(value)
    stress = product(
        (high_ref[...], low_ref[...]), (steps_high[...], steps_low[...]), NT
    )
    for owner in range(SHARES):
        for tile in range(SLOW // LANES):
            out_ref[owner, pl.ds(tile * OWNED, OWNED), :] = stress[
                owner * OWNED : (owner + 1) * OWNED, tile * LANES : (tile + 1) * LANES
            ]


def plus(a, b):
    return a[0] + b[0], a[1] + b[1]


def minus(a, b):
    return a[0] - b[0], a[1] - b[1]


def by_minus_i(a):
    return a[1], -a[0]


def times(a, real, imag):
    return a[0] * real - a[1] * imag, a[0] * imag + a[1] * real


def transform(values):
    size = len(values)
    if size == 1:
        return values
    even, odd = transform(values[::2]), transform(values[1::2])
    low, high = [], []
    for k in range(size // 2):
        turned = odd[k]
        if 4 * k == size:
            turned = by_minus_i(turned)
        elif k:
            turned = times(
                turned,
                float(np.cos(2 * np.pi * k / size)),
                float(-np.sin(2 * np.pi * k / size)),
            )
        low.append(plus(even[k], turned))
        high.append(minus(even[k], turned))
    return low + high


def spectra(got_ref, high_ref, low_ref, twist_ref, out_ref, rows_high, rows_low, stage):
    for n2 in range(FAST):
        for tile in range(SLOW // LANES):
            at = (pl.ds(n2 * PADDED, OWNED), pl.ds(tile * LANES, LANES))
            value = got_ref[n2, pl.ds(tile * OWNED, OWNED), :]
            rows_high[at], rows_low[at] = split(value)
    stage[...] = product(
        (rows_high[...], rows_low[...]), (high_ref[...], low_ref[...]), NN
    )
    tiles = STEPS // 2 // LANES
    for top in range(0, OWNED, 8):
        for left in range(0, SLOW, LANES):
            values = []
            for n2 in range(FAST):
                rows = pl.ds(n2 * PADDED + top, 8)
                value = (
                    stage[rows, pl.ds(left, LANES)],
                    stage[rows, pl.ds(SLOW + left, LANES)],
                )
                if n2:
                    lanes = pl.ds(left, LANES)
                    value = times(
                        value,
                        twist_ref[0, pl.ds(n2, 1), lanes],
                        twist_ref[1, pl.ds(n2, 1), lanes],
                    )
                values.append(value)
            valid = min(8, OWNED - top)
            for k2, value in enumerate(transform(values)[: FAST // 2]):
                tile = (k2 * SLOW + left) // LANES
                for part in range(2):
                    first = (top * tiles + tile) * 2 + part
                    to = pl.ds(first, valid, stride=2 * tiles)
                    out_ref[to, :] = value[part][:valid]


def call(kernel, shapes, *args, scratch=(), flops=0):
    whole = pl.BlockSpec(memory_space=pltpu.VMEM)
    return pl.pallas_call(
        kernel,
        out_shape=shapes,
        in_specs=[whole] * len(args),
        out_specs=jax.tree.map(lambda _: whole, shapes),
        scratch_shapes=scratch,
        compiler_params=pltpu.CompilerParams(vmem_limit_bytes=8 << 20),
        cost_estimate=pl.CostEstimate(
            flops=flops,
            transcendentals=0,
            bytes_accessed=sum(a.size * a.dtype.itemsize for a in args),
        ),
    )(*args)


def swap(x, axis):
    return lax.ppermute(x, axis, [(0, 1), (1, 0)])


def per_device(modal_history, stress_modes):
    modes, width = stress_modes.shape
    shape = jax.ShapeDtypeStruct
    vmem = pltpu.VMEM
    sent = call(
        scatter_steps,
        shape((SHARES * BLOCKS * 2, LANES), f32),
        modal_history.T,
        scratch=[vmem((LANES, LANES), f32)] * 2,
    )
    got = lax.all_to_all(
        sent.reshape(SHARES * BLOCKS, 2, LANES),
        MODE + ELEM,
        split_axis=0,
        concat_axis=0,
        tiled=True,
    )
    near = [stress_modes] + [
        lax.ppermute(stress_modes, "x", [(i, (i + k) % 4) for i in range(4)])
        for k in (1, 2, 3)
    ]
    near = jnp.concatenate(near)
    across = [(i, i ^ 3) for i in range(4)]
    high, low = call(
        order_modes,
        (shape((width, MODES), bf16), shape((width, MODES), bf16)),
        near,
        swap(near, "yh"),
        swap(near, "c"),
        lax.ppermute(near, ("yh", "c"), across),
        scratch=[vmem((MODES, width), f32)],
    )
    stress = call(
        contract,
        shape((SHARES, SLOW // LANES * OWNED, LANES), f32),
        high,
        low,
        got.reshape(SHARES * BLOCKS * 2, LANES),
        scratch=[vmem((SLOW, MODES), bf16)] * 2,
    )
    owned = lax.all_to_all(stress, MODE, split_axis=0, concat_axis=0, tiled=True)
    first_high, first_low, twist = tables()
    rows = FAST * PADDED
    out = call(
        spectra,
        shape((OWNED * STEPS // LANES, LANES), f32),
        owned,
        first_high,
        first_low,
        twist,
        scratch=[vmem((rows, SLOW), bf16)] * 2 + [vmem((rows, 2 * SLOW), f32)],
    )
    out = out.reshape(OWNED, STEPS // 2 // LANES, 2, LANES).transpose(0, 2, 1, 3)
    return out.reshape(OWNED, 2, STEPS // 2)


def solution(mesh):
    parts = Mesh(mesh.devices.reshape(SIZES), PARTS)
    return jax.shard_map(
        per_device,
        mesh=parts,
        in_specs=(P(ELEM, MODE), P(MODE, ELEM)),
        out_specs=P(PARTS, None, None),
        check_vma=False,
    )
```

```python
import numpy as np

import jax
import jax.numpy as jnp
from jax import lax
from jax.experimental import pallas as pl
from jax.experimental.pallas import tpu as pltpu
from jax.sharding import Mesh, PartitionSpec as P

PARTS = ("z", "yl", "x", "yh", "c")
SIZES = (8, 4, 4, 2, 2)
ELEM = ("z", "yl")
MODE = ("x", "yh", "c")
PAIR = ("x", "c")
BLOCKS, SHARES, PAIRS = 32, 16, 8
STEPS, MODES = 4096, 256
SLOW, FAST = 256, 16
OWNED, PADDED = 12, 16
LANES = 128
f32, bf16 = jnp.float32, jnp.bfloat16
NN = (((1,), (0,)), ((), ()))
NT = (((1,), (1,)), ((), ()))


def split(x):
    high = x.astype(bf16)
    return high, (x - high.astype(f32)).astype(bf16)


def product(a, b, dims):
    (ah, al), (bh, bl) = a, b
    dot = lambda x, y: lax.dot_general(x, y, dims, preferred_element_type=f32)
    return dot(ah, bh) + (dot(ah, bl) + dot(al, bh))


def tables():
    k1 = np.arange(SLOW)
    angle = 2.0 * np.pi * ((k1[:, None] * k1[None, :]) % SLOW) / SLOW
    first = np.concatenate([np.cos(angle), -np.sin(angle)], axis=1) / np.sqrt(STEPS)
    high = first.astype(np.float32).astype(jnp.bfloat16)
    low = (first - high.astype(np.float64)).astype(jnp.bfloat16)
    turn = 2.0 * np.pi * (np.arange(FAST)[:, None] * k1[None, :]) / STEPS
    twist = np.stack([np.cos(turn), -np.sin(turn)])
    return high, low, twist.astype(np.float32)


def scatter(history_hbm, modes_hbm, out_ref, wide, tall, modes_ref, arrived):
    modes, width = modes_ref.shape
    wide[...] = jnp.zeros_like(wide)
    at = pl.multiple_of(lax.rem(lax.axis_index(PAIR), LANES // modes) * modes, modes)
    copies = (
        pltpu.make_async_copy(history_hbm, wide.at[pl.ds(at, modes), :], arrived.at[0]),
        pltpu.make_async_copy(modes_hbm, modes_ref, arrived.at[1]),
    )
    for copy in copies:
        copy.start()
    for copy in copies:
        copy.wait()
    tall[...] = wide[...].T
    half = modes // 2
    for pair in range(PAIRS):
        for high in range(2):
            rows = tall[pl.ds(8 * high + pair, LANES // FAST, stride=FAST), :]
            out_ref[pair, pl.ds(high * 8, 8), :] = rows
        first = (pair % 2) * half
        out_ref[pair, pl.ds(16, half), :] = modes_ref[pl.ds(first, half), :LANES]
        rest = width - LANES
        for side in range(2):
            out_ref[pair, pl.ds(16 + half, 8), pl.ds(side * rest, rest)] = modes_ref[
                pl.ds(first + side * 8, 8), LANES:
            ]


def spread(got_ref, out_ref):
    for quad in range(PAIRS // 4):
        joined = None
        for sender in range(4 * quad, 4 * quad + 4):
            rows = got_ref[sender, pl.ds(0, 16), :]
            joined = rows if joined is None else joined + rows
        lanes = pl.ds(quad * LANES, LANES)
        out_ref[:, :, lanes] = jnp.broadcast_to(joined, (BLOCKS,) + joined.shape)


def order_modes(own_ref, other_ref, high_ref, low_ref, whole):
    c = lax.axis_index("c")
    half = MODES // PAIRS // 2
    rest = whole.shape[1] - LANES
    for ref, which in ((own_ref, c), (other_ref, 1 - c)):
        for sender in range(PAIRS):
            at = pl.multiple_of(sender * 2 * half + which * half, half)
            whole[pl.ds(at, half), pl.ds(0, LANES)] = ref[sender, pl.ds(0, half), :]
            for side in range(2):
                rows = pl.ds(pl.multiple_of(at + side * 8, 8), 8)
                whole[rows, pl.ds(LANES, rest)] = ref[
                    sender, pl.ds(half, 8), pl.ds(side * rest, rest)
                ]
    high_ref[...], low_ref[...] = split(whole[...].T)


def contract(high_ref, low_ref, steps_ref, out_ref):
    modes = (high_ref[...], low_ref[...])
    tiles = SLOW // LANES
    for high in range(2):
        steps = steps_ref[:, pl.ds(8 * high, 8), :].reshape(SLOW, MODES)
        stress = product(modes, split(steps), NT)
        for owner in range(SHARES):
            for tile in range(tiles):
                out_ref[owner, pl.ds((high * tiles + tile) * OWNED, OWNED), :] = stress[
                    owner * OWNED : (owner + 1) * OWNED,
                    tile * LANES : (tile + 1) * LANES,
                ]


def plus(a, b):
    return a[0] + b[0], a[1] + b[1]


def minus(a, b):
    return a[0] - b[0], a[1] - b[1]


def by_minus_i(a):
    return a[1], -a[0]


def times(a, real, imag):
    return a[0] * real - a[1] * imag, a[0] * imag + a[1] * real


def transform(values):
    size = len(values)
    if size == 1:
        return values
    even, odd = transform(values[::2]), transform(values[1::2])
    low, high = [], []
    for k in range(size // 2):
        turned = odd[k]
        if 4 * k == size:
            turned = by_minus_i(turned)
        elif k:
            turned = times(
                turned,
                float(np.cos(2 * np.pi * k / size)),
                float(-np.sin(2 * np.pi * k / size)),
            )
        low.append(plus(even[k], turned))
        high.append(minus(even[k], turned))
    return low + high


def spectra(got_ref, high_ref, low_ref, twist_ref, out_ref, rows_high, rows_low, stage):
    for n2 in range(FAST):
        for tile in range(SLOW // LANES):
            at = (pl.ds(n2 * PADDED, OWNED), pl.ds(tile * LANES, LANES))
            sender = (n2 % 8) // 2 * 4 + n2 % 2
            part = pl.ds((n2 // 8 * 2 + tile) * OWNED, OWNED)
            value = got_ref[sender, part, :] + got_ref[sender + 2, part, :]
            rows_high[at], rows_low[at] = split(value)
    stage[...] = product(
        (rows_high[...], rows_low[...]), (high_ref[...], low_ref[...]), NN
    )
    tiles = STEPS // 2 // LANES
    for top in range(0, OWNED, 8):
        for left in range(0, SLOW, LANES):
            values = []
            for n2 in range(FAST):
                rows = pl.ds(n2 * PADDED + top, 8)
                value = (
                    stage[rows, pl.ds(left, LANES)],
                    stage[rows, pl.ds(SLOW + left, LANES)],
                )
                if n2:
                    lanes = pl.ds(left, LANES)
                    value = times(
                        value,
                        twist_ref[0, pl.ds(n2, 1), lanes],
                        twist_ref[1, pl.ds(n2, 1), lanes],
                    )
                values.append(value)
            valid = min(8, OWNED - top)
            for k2, value in enumerate(transform(values)[: FAST // 2]):
                tile = (k2 * SLOW + left) // LANES
                for part in range(2):
                    first = (top * tiles + tile) * 2 + part
                    to = pl.ds(first, valid, stride=2 * tiles)
                    out_ref[to, :] = value[part][:valid]


def call(kernel, shapes, *args, scratch=(), space=pltpu.VMEM, limit=8 << 20):
    whole = pl.BlockSpec(memory_space=pltpu.VMEM)
    return pl.pallas_call(
        kernel,
        out_shape=shapes,
        in_specs=[pl.BlockSpec(memory_space=space)] * len(args),
        out_specs=jax.tree.map(lambda _: whole, shapes),
        scratch_shapes=scratch,
        compiler_params=pltpu.CompilerParams(vmem_limit_bytes=limit),
        cost_estimate=pl.CostEstimate(
            flops=0,
            transcendentals=0,
            bytes_accessed=sum(a.size * a.dtype.itemsize for a in args),
        ),
    )(*args)


def per_device(modal_history, stress_modes):
    modes, width = stress_modes.shape
    shape = jax.ShapeDtypeStruct
    vmem = pltpu.VMEM
    sent = call(
        scatter,
        shape((PAIRS, 16 + 24, LANES), f32),
        modal_history.T,
        stress_modes,
        scratch=[vmem((LANES, LANES), f32)] * 2
        + [vmem((modes, width), f32), pltpu.SemaphoreType.DMA((2,))],
        space=pltpu.HBM,
        limit=60 << 20,
    )
    got = lax.all_to_all(sent, PAIR, split_axis=0, concat_axis=0, tiled=True)
    history = call(spread, shape((BLOCKS, 16, MODES), f32), got)
    steps = lax.all_to_all(history, ELEM, split_axis=0, concat_axis=0, tiled=True)
    own = got[:, 16:]
    high, low = call(
        order_modes,
        (shape((width, MODES), bf16), shape((width, MODES), bf16)),
        own,
        lax.ppermute(own, "c", [(0, 1), (1, 0)]),
        scratch=[vmem((MODES, width), f32)],
    )
    stress = call(
        contract,
        shape((SHARES, 2 * SLOW // LANES * OWNED, LANES), f32),
        high,
        low,
        steps,
    )
    owned = lax.all_to_all(stress, MODE, split_axis=0, concat_axis=0, tiled=True)
    first_high, first_low, twist = tables()
    rows = FAST * PADDED
    out = call(
        spectra,
        shape((OWNED * STEPS // LANES, LANES), f32),
        owned,
        first_high,
        first_low,
        twist,
        scratch=[vmem((rows, SLOW), bf16)] * 2 + [vmem((rows, 2 * SLOW), f32)],
    )
    out = out.reshape(OWNED, STEPS // 2 // LANES, 2, LANES).transpose(0, 2, 1, 3)
    return out.reshape(OWNED, 2, STEPS // 2)


def solution(mesh):
    parts = Mesh(mesh.devices.reshape(SIZES), PARTS)
    return jax.shard_map(
        per_device,
        mesh=parts,
        in_specs=(P(ELEM, MODE), P(MODE, ELEM)),
        out_specs=P(PARTS, None, None),
        check_vma=False,
    )
```

```python
import numpy as np

import jax
import jax.numpy as jnp
from jax import lax
from jax.experimental import pallas as pl
from jax.experimental.pallas import tpu as pltpu
from jax.sharding import Mesh, PartitionSpec as P

PARTS = ("z", "ya", "yb", "x", "yh", "c")
SIZES = (8, 2, 2, 4, 2, 2)
ELEM = ("z", "ya", "yb")
MODE = ("x", "yh", "c")
PAIR = ("x", "c")
PLANE = ("z", "ya")
LAST = ("yh", "c", "x", "yb")
BLOCKS, SHARES, PAIRS = 16, 16, 8
STEPS, MODES = 4096, 256
SLOW, FAST = 256, 16
OWNED, PADDED = 12, 16
LANES = 128
f32, bf16 = jnp.float32, jnp.bfloat16
NN = (((1,), (0,)), ((), ()))
NT = (((1,), (1,)), ((), ()))


def split(x):
    high = x.astype(bf16)
    return high, (x - high.astype(f32)).astype(bf16)


def product(a, b, dims):
    (ah, al), (bh, bl) = a, b
    dot = lambda x, y: lax.dot_general(x, y, dims, preferred_element_type=f32)
    return dot(ah, bh) + (dot(ah, bl) + dot(al, bh))


def tables():
    k1 = np.arange(SLOW)
    angle = 2.0 * np.pi * ((k1[:, None] * k1[None, :]) % SLOW) / SLOW
    first = np.concatenate([np.cos(angle), -np.sin(angle)], axis=1) / np.sqrt(STEPS)
    first = first.reshape(BLOCKS, 2, 8, 2 * SLOW).transpose(1, 0, 2, 3)
    first = first.reshape(SLOW, 2 * SLOW)
    high = first.astype(np.float32).astype(jnp.bfloat16)
    low = (first - high.astype(np.float64)).astype(jnp.bfloat16)
    turn = 2.0 * np.pi * (np.arange(FAST)[:, None] * k1[None, :]) / STEPS
    twist = np.stack([np.cos(turn), -np.sin(turn)])
    return high, low, twist.astype(np.float32)


def scatter(history_hbm, modes_hbm, out_ref, wide, tall, modes_ref, arrived):
    modes, width = modes_ref.shape
    wide[...] = jnp.zeros_like(wide)
    at = pl.multiple_of(lax.rem(lax.axis_index(PAIR), LANES // modes) * modes, modes)
    copies = (
        pltpu.make_async_copy(history_hbm, wide.at[pl.ds(at, modes), :], arrived.at[0]),
        pltpu.make_async_copy(modes_hbm, modes_ref, arrived.at[1]),
    )
    for copy in copies:
        copy.start()
    for copy in copies:
        copy.wait()
    tall[...] = wide[...].T
    half = modes // 2
    rest = width - LANES
    for pair in range(PAIRS):
        for high in range(2):
            rows = tall[pl.ds(8 * high + pair, LANES // FAST, stride=FAST), :]
            out_ref[pair, pl.ds(high * 8, 8), :] = rows
        out_ref[pair, pl.ds(16, modes), :] = modes_ref[:, :LANES]
        for side in range(2):
            to = (pair, pl.ds(16 + modes, half), pl.ds(side * rest, rest))
            out_ref[to] = modes_ref[pl.ds(side * half, half), LANES:]


def spread(got_ref, out_ref):
    for quad in range(PAIRS // 4):
        joined = None
        for sender in range(4 * quad, 4 * quad + 4):
            rows = got_ref[sender, pl.ds(0, 16), :]
            joined = rows if joined is None else joined + rows
        lanes = pl.ds(quad * LANES, LANES)
        out_ref[:, :, lanes] = jnp.broadcast_to(joined, (BLOCKS,) + joined.shape)


def order_modes(own_ref, other_ref, high_ref, low_ref, whole):
    yb = lax.axis_index("yb")
    modes = MODES // PAIRS
    half = modes // 2
    width = whole.shape[1]
    rest = width - LANES
    for ref, which in ((own_ref, yb), (other_ref, 1 - yb)):
        for sender in range(PAIRS):
            at = sender * modes
            whole[pl.ds(at, modes), :LANES] = ref[sender, pl.ds(0, modes), :]
            for side in range(2):
                whole[pl.ds(at + side * half, half), LANES:] = ref[
                    sender, pl.ds(modes, half), pl.ds(side * rest, rest)
                ]
        to = (pl.ds(pl.multiple_of(which * width, width), width), slice(None))
        high_ref[to], low_ref[to] = split(whole[...].T)


def last_index(yh, c, x, yb):
    return ((yh * 2 + c) * 4 + x) * 2 + yb


def contract(high_ref, low_ref, steps_ref, out_ref):
    steps = [
        steps_ref[:, pl.ds(8 * high, 8), :].reshape(LANES, MODES) for high in range(2)
    ]
    stress = product(
        (high_ref[...], low_ref[...]), split(jnp.concatenate(steps)), NT
    )
    for yb in range(2):
        for share in range(SHARES):
            owner = last_index(share // 2 % 2, share % 2, share // 4, yb)
            first = (yb * SHARES + share) * OWNED
            for high in range(2):
                out_ref[owner, pl.ds(high * OWNED, OWNED), :] = stress[
                    first : first + OWNED, high * LANES : (high + 1) * LANES
                ]


def plus(a, b):
    return a[0] + b[0], a[1] + b[1]


def minus(a, b):
    return a[0] - b[0], a[1] - b[1]


def by_minus_i(a):
    return a[1], -a[0]


def times(a, real, imag):
    return a[0] * real - a[1] * imag, a[0] * imag + a[1] * real


def transform(values):
    size = len(values)
    if size == 1:
        return values
    even, odd = transform(values[::2]), transform(values[1::2])
    low, high = [], []
    for k in range(size // 2):
        turned = odd[k]
        if 4 * k == size:
            turned = by_minus_i(turned)
        elif k:
            turned = times(
                turned,
                float(np.cos(2 * np.pi * k / size)),
                float(-np.sin(2 * np.pi * k / size)),
            )
        low.append(plus(even[k], turned))
        high.append(minus(even[k], turned))
    return low + high


def spectra(got_ref, high_ref, low_ref, twist_ref, out_ref, rows_high, rows_low, stage):
    for n2 in range(FAST):
        for yb in range(2):
            at = (pl.ds(n2 * PADDED, OWNED), pl.ds(yb * LANES, LANES))
            rows = pl.ds(n2 // 8 * OWNED, OWNED)
            x, c = n2 % 8 // 2, n2 % 2
            low = got_ref[last_index(0, c, x, yb), rows, :]
            value = low + got_ref[last_index(1, c, x, yb), rows, :]
            rows_high[at], rows_low[at] = split(value)
    stage[...] = product(
        (rows_high[...], rows_low[...]), (high_ref[...], low_ref[...]), NN
    )
    tiles = STEPS // 2 // LANES
    for top in range(0, OWNED, 8):
        for left in range(0, SLOW, LANES):
            values = []
            for n2 in range(FAST):
                rows = pl.ds(n2 * PADDED + top, 8)
                value = (
                    stage[rows, pl.ds(left, LANES)],
                    stage[rows, pl.ds(SLOW + left, LANES)],
                )
                if n2:
                    lanes = pl.ds(left, LANES)
                    value = times(
                        value,
                        twist_ref[0, pl.ds(n2, 1), lanes],
                        twist_ref[1, pl.ds(n2, 1), lanes],
                    )
                values.append(value)
            valid = min(8, OWNED - top)
            for k2, value in enumerate(transform(values)[: FAST // 2]):
                tile = (k2 * SLOW + left) // LANES
                for part in range(2):
                    first = (top * tiles + tile) * 2 + part
                    to = pl.ds(first, valid, stride=2 * tiles)
                    out_ref[to, :] = value[part][:valid]


def call(kernel, shapes, *args, scratch=(), space=pltpu.VMEM, limit=8 << 20):
    whole = pl.BlockSpec(memory_space=pltpu.VMEM)
    return pl.pallas_call(
        kernel,
        out_shape=shapes,
        in_specs=[pl.BlockSpec(memory_space=space)] * len(args),
        out_specs=jax.tree.map(lambda _: whole, shapes),
        scratch_shapes=scratch,
        compiler_params=pltpu.CompilerParams(vmem_limit_bytes=limit),
        cost_estimate=pl.CostEstimate(
            flops=0,
            transcendentals=0,
            bytes_accessed=sum(a.size * a.dtype.itemsize for a in args),
        ),
    )(*args)


def per_device(modal_history, stress_modes):
    modes, width = stress_modes.shape
    shape = jax.ShapeDtypeStruct
    vmem = pltpu.VMEM
    sent = call(
        scatter,
        shape((PAIRS, 16 + 48, LANES), f32),
        modal_history.T,
        stress_modes,
        scratch=[vmem((LANES, LANES), f32)] * 2
        + [vmem((modes, width), f32), pltpu.SemaphoreType.DMA((2,))],
        space=pltpu.HBM,
        limit=60 << 20,
    )
    got = lax.all_to_all(sent, PAIR, split_axis=0, concat_axis=0, tiled=True)
    history = call(spread, shape((BLOCKS, 16, MODES), f32), got)
    steps = lax.all_to_all(history, PLANE, split_axis=0, concat_axis=0, tiled=True)
    own = got[:, 16:]
    high, low = call(
        order_modes,
        (shape((2 * width, MODES), bf16), shape((2 * width, MODES), bf16)),
        own,
        lax.ppermute(own, "yb", [(0, 1), (1, 0)]),
        scratch=[vmem((MODES, width), f32)],
    )
    stress = call(
        contract,
        shape((2 * SHARES, 2 * OWNED, LANES), f32),
        high,
        low,
        steps,
    )
    owned = lax.all_to_all(stress, LAST, split_axis=0, concat_axis=0, tiled=True)
    first_high, first_low, twist = tables()
    rows = FAST * PADDED
    out = call(
        spectra,
        shape((OWNED * STEPS // LANES, LANES), f32),
        owned,
        first_high,
        first_low,
        twist,
        scratch=[vmem((rows, SLOW), bf16)] * 2 + [vmem((rows, 2 * SLOW), f32)],
    )
    out = out.reshape(OWNED, STEPS // 2 // LANES, 2, LANES).transpose(0, 2, 1, 3)
    return out.reshape(OWNED, 2, STEPS // 2)


def solution(mesh):
    parts = Mesh(mesh.devices.reshape(SIZES), PARTS)
    return jax.shard_map(
        per_device,
        mesh=parts,
        in_specs=(P(ELEM, MODE), P(MODE, ELEM)),
        out_specs=P(PARTS, None, None),
        check_vma=False,
    )
```

```python
import numpy as np

import jax
import jax.numpy as jnp
from jax import lax
from jax.experimental import pallas as pl
from jax.experimental.pallas import tpu as pltpu
from jax.sharding import Mesh, PartitionSpec as P

PARTS = ("z2", "z1", "z0", "y1", "y0", "x1", "x0", "y2", "c")
SIZES = (2,) * 9
ELEM = ("z2", "z1", "z0", "y1", "y0")
MODE = ("x1", "x0", "y2", "c")
PAIR = ("x1", "x0", "c")
PLANE = ("y1", "z2", "z1", "z0")
SIDE = "y0"
LAST = ("y2", "y0", "c", "x1", "x0")
BLOCKS, SHARES, PAIRS = 16, 16, 8
STEPS, MODES = 4096, 256
SLOW, FAST = 256, 16
OWNED, PADDED = 12, 16
LANES = 128
f32, bf16 = jnp.float32, jnp.bfloat16
NN = (((1,), (0,)), ((), ()))
NT = (((1,), (1,)), ((), ()))


def split(x):
    high = x.astype(bf16)
    return high, (x - high.astype(f32)).astype(bf16)


def product(a, b, dims):
    (ah, al), (bh, bl) = a, b
    dot = lambda x, y: lax.dot_general(x, y, dims, preferred_element_type=f32)
    return dot(ah, bh) + (dot(ah, bl) + dot(al, bh))


def tables():
    k1 = np.arange(SLOW)
    angle = 2.0 * np.pi * ((k1[:, None] * k1[None, :]) % SLOW) / SLOW
    first = np.concatenate([np.cos(angle), -np.sin(angle)], axis=1) / np.sqrt(STEPS)
    first = first.reshape(2 * BLOCKS, 8, 2 * SLOW)
    order = [
        index_of(ELEM, **{SIDE: side}, **place) for side in range(2) for place in places(PLANE)
    ]
    first = first[np.array(order)].reshape(SLOW, 2 * SLOW)
    high = first.astype(np.float32).astype(jnp.bfloat16)
    low = (first - high.astype(np.float64)).astype(jnp.bfloat16)
    turn = 2.0 * np.pi * (np.arange(FAST)[:, None] * k1[None, :]) / STEPS
    twist = np.stack([np.cos(turn), -np.sin(turn)])
    return high, low, twist.astype(np.float32)


def scatter(history_hbm, modes_hbm, out_ref, wide, tall, modes_ref, arrived):
    modes, width = modes_ref.shape
    wide[...] = jnp.zeros_like(wide)
    at = pl.multiple_of(lax.rem(lax.axis_index(PAIR), LANES // modes) * modes, modes)
    copies = (
        pltpu.make_async_copy(history_hbm, wide.at[pl.ds(at, modes), :], arrived.at[0]),
        pltpu.make_async_copy(modes_hbm, modes_ref, arrived.at[1]),
    )
    for copy in copies:
        copy.start()
    for copy in copies:
        copy.wait()
    tall[...] = wide[...].T
    half = modes // 2
    rest = width - LANES
    for pair in range(PAIRS):
        for high in range(2):
            rows = tall[pl.ds(8 * high + pair, LANES // FAST, stride=FAST), :]
            out_ref[pair, pl.ds(high * 8, 8), :] = rows
        out_ref[pair, pl.ds(16, modes), :] = modes_ref[:, :LANES]
        for part in range(2):
            to = (pair, pl.ds(16 + modes, half), pl.ds(part * rest, rest))
            out_ref[to] = modes_ref[pl.ds(part * half, half), LANES:]


def spread(got_ref, out_ref):
    for quad in range(PAIRS // 4):
        joined = None
        for sender in range(4 * quad, 4 * quad + 4):
            rows = got_ref[sender, pl.ds(0, 16), :]
            joined = rows if joined is None else joined + rows
        lanes = pl.ds(quad * LANES, LANES)
        out_ref[:, :, lanes] = jnp.broadcast_to(joined, (BLOCKS,) + joined.shape)


def order_modes(own_ref, other_ref, high_ref, low_ref, whole):
    side = lax.axis_index(SIDE)
    modes = MODES // PAIRS
    half = modes // 2
    width = whole.shape[1]
    rest = width - LANES
    for ref, which in ((own_ref, side), (other_ref, 1 - side)):
        for sender in range(PAIRS):
            at = sender * modes
            whole[pl.ds(at, modes), :LANES] = ref[sender, pl.ds(0, modes), :]
            for part in range(2):
                whole[pl.ds(at + part * half, half), LANES:] = ref[
                    sender, pl.ds(modes, half), pl.ds(part * rest, rest)
                ]
        to = (pl.ds(pl.multiple_of(which * width, width), width), slice(None))
        high_ref[to], low_ref[to] = split(whole[...].T)


def index_of(axes, **at):
    index = 0
    for axis in axes:
        index = index * dict(zip(PARTS, SIZES))[axis] + at[axis]
    return index


def places(axes):
    sizes = dict(zip(PARTS, SIZES))
    grid = np.indices([sizes[a] for a in axes]).reshape(len(axes), -1)
    return [dict(zip(axes, map(int, column))) for column in grid.T]


def contract(high_ref, low_ref, steps_ref, out_ref):
    steps = [
        steps_ref[:, pl.ds(8 * high, 8), :].reshape(LANES, MODES) for high in range(2)
    ]
    stress = product(
        (high_ref[...], low_ref[...]), split(jnp.concatenate(steps)), NT
    )
    for side in range(2):
        for share in range(SHARES):
            owner = index_of(LAST, **{SIDE: side}, **places(MODE)[share])
            first = (side * SHARES + share) * OWNED
            for high in range(2):
                out_ref[owner, pl.ds(high * OWNED, OWNED), :] = stress[
                    first : first + OWNED, high * LANES : (high + 1) * LANES
                ]


def plus(a, b):
    return a[0] + b[0], a[1] + b[1]


def minus(a, b):
    return a[0] - b[0], a[1] - b[1]


def by_minus_i(a):
    return a[1], -a[0]


def times(a, real, imag):
    return a[0] * real - a[1] * imag, a[0] * imag + a[1] * real


def transform(values):
    size = len(values)
    if size == 1:
        return values
    even, odd = transform(values[::2]), transform(values[1::2])
    low, high = [], []
    for k in range(size // 2):
        turned = odd[k]
        if 4 * k == size:
            turned = by_minus_i(turned)
        elif k:
            turned = times(
                turned,
                float(np.cos(2 * np.pi * k / size)),
                float(-np.sin(2 * np.pi * k / size)),
            )
        low.append(plus(even[k], turned))
        high.append(minus(even[k], turned))
    return low + high


def spectra(got_ref, high_ref, low_ref, twist_ref, out_ref, rows_high, rows_low, stage):
    for n2 in range(FAST):
        for side in range(2):
            at = (pl.ds(n2 * PADDED, OWNED), pl.ds(side * LANES, LANES))
            rows = pl.ds(n2 // 8 * OWNED, OWNED)
            place = places(PAIR)[n2 % 8]
            senders = [index_of(LAST, **{SIDE: side}, y2=y2, **place) for y2 in range(2)]
            value = got_ref[senders[0], rows, :] + got_ref[senders[1], rows, :]
            rows_high[at], rows_low[at] = split(value)
    stage[...] = product(
        (rows_high[...], rows_low[...]), (high_ref[...], low_ref[...]), NN
    )
    tiles = STEPS // 2 // LANES
    for top in range(0, OWNED, 8):
        for left in range(0, SLOW, LANES):
            values = []
            for n2 in range(FAST):
                rows = pl.ds(n2 * PADDED + top, 8)
                value = (
                    stage[rows, pl.ds(left, LANES)],
                    stage[rows, pl.ds(SLOW + left, LANES)],
                )
                if n2:
                    lanes = pl.ds(left, LANES)
                    value = times(
                        value,
                        twist_ref[0, pl.ds(n2, 1), lanes],
                        twist_ref[1, pl.ds(n2, 1), lanes],
                    )
                values.append(value)
            valid = min(8, OWNED - top)
            for k2, value in enumerate(transform(values)[: FAST // 2]):
                tile = (k2 * SLOW + left) // LANES
                for part in range(2):
                    first = (top * tiles + tile) * 2 + part
                    to = pl.ds(first, valid, stride=2 * tiles)
                    out_ref[to, :] = value[part][:valid]


def call(kernel, shapes, *args, scratch=(), space=pltpu.VMEM, limit=8 << 20):
    whole = pl.BlockSpec(memory_space=pltpu.VMEM)
    return pl.pallas_call(
        kernel,
        out_shape=shapes,
        in_specs=[pl.BlockSpec(memory_space=space)] * len(args),
        out_specs=jax.tree.map(lambda _: whole, shapes),
        scratch_shapes=scratch,
        compiler_params=pltpu.CompilerParams(vmem_limit_bytes=limit),
        cost_estimate=pl.CostEstimate(
            flops=0,
            transcendentals=0,
            bytes_accessed=sum(a.size * a.dtype.itemsize for a in args),
        ),
    )(*args)


def per_device(modal_history, stress_modes):
    modes, width = stress_modes.shape
    shape = jax.ShapeDtypeStruct
    vmem = pltpu.VMEM
    sent = call(
        scatter,
        shape((PAIRS, 16 + 48, LANES), f32),
        modal_history.T,
        stress_modes,
        scratch=[vmem((LANES, LANES), f32)] * 2
        + [vmem((modes, width), f32), pltpu.SemaphoreType.DMA((2,))],
        space=pltpu.HBM,
        limit=60 << 20,
    )
    got = lax.all_to_all(sent, PAIR, split_axis=0, concat_axis=0, tiled=True)
    history = call(spread, shape((BLOCKS, 16, MODES), f32), got)
    steps = lax.all_to_all(history, PLANE, split_axis=0, concat_axis=0, tiled=True)
    own = got[:, 16:]
    high, low = call(
        order_modes,
        (shape((2 * width, MODES), bf16), shape((2 * width, MODES), bf16)),
        own,
        lax.ppermute(own, SIDE, [(0, 1), (1, 0)]),
        scratch=[vmem((MODES, width), f32)],
    )
    stress = call(
        contract,
        shape((2 * SHARES, 2 * OWNED, LANES), f32),
        high,
        low,
        steps,
    )
    owned = lax.all_to_all(stress, LAST, split_axis=0, concat_axis=0, tiled=True)
    first_high, first_low, twist = tables()
    rows = FAST * PADDED
    out = call(
        spectra,
        shape((OWNED * STEPS // LANES, LANES), f32),
        owned,
        first_high,
        first_low,
        twist,
        scratch=[vmem((rows, SLOW), bf16)] * 2 + [vmem((rows, 2 * SLOW), f32)],
    )
    out = out.reshape(OWNED, STEPS // 2 // LANES, 2, LANES).transpose(0, 2, 1, 3)
    return out.reshape(OWNED, 2, STEPS // 2)


def solution(mesh):
    parts = Mesh(mesh.devices.reshape(SIZES), PARTS)
    return jax.shard_map(
        per_device,
        mesh=parts,
        in_specs=(P(ELEM, MODE), P(MODE, ELEM)),
        out_specs=P(PARTS, None, None),
        check_vma=False,
    )
```

```python
import numpy as np

import jax
import jax.numpy as jnp
from jax import lax
from jax.experimental import pallas as pl
from jax.experimental.pallas import tpu as pltpu
from jax.sharding import Mesh, PartitionSpec as P

PARTS = ("z2", "z1", "z0", "y1", "y0", "x1", "x0", "y2", "c")
SIZES = (2,) * 9
ELEM = ("z2", "z1", "z0", "y1", "y0")
MODE = ("x1", "x0", "y2", "c")
PAIR = ("x1", "x0", "c")
PLANE = ("y1", "z2", "z1", "z0")
SIDE = "y0"
LAST = ("y2", "y0", "c", "x1", "x0")
BLOCKS, SHARES, PAIRS = 16, 16, 8
STEPS, MODES = 4096, 256
SLOW, FAST = 256, 16
OWNED, PADDED = 12, 16
LANES = 128
f32, bf16 = jnp.float32, jnp.bfloat16
NN = (((1,), (0,)), ((), ()))
NT = (((1,), (1,)), ((), ()))


def split(x):
    high = x.astype(bf16)
    return high, (x - high.astype(f32)).astype(bf16)


def product(a, b, dims):
    (ah, al), (bh, bl) = a, b
    dot = lambda x, y: lax.dot_general(x, y, dims, preferred_element_type=f32)
    return dot(ah, bh) + (dot(ah, bl) + dot(al, bh))


def tables():
    k1 = np.arange(SLOW)
    angle = 2.0 * np.pi * ((k1[:, None] * k1[None, :]) % SLOW) / SLOW
    first = np.concatenate([np.cos(angle), -np.sin(angle)], axis=1) / np.sqrt(STEPS)
    first = first.reshape(2 * BLOCKS, 8, 2 * SLOW)
    order = [
        index_of(ELEM, **{SIDE: side}, **place) for side in range(2) for place in places(PLANE)
    ]
    first = first[np.array(order)].reshape(SLOW, 2 * SLOW)
    high = first.astype(np.float32).astype(jnp.bfloat16)
    low = (first - high.astype(np.float64)).astype(jnp.bfloat16)
    turn = 2.0 * np.pi * (np.arange(FAST)[:, None] * k1[None, :]) / STEPS
    twist = np.stack([np.cos(turn), -np.sin(turn)])
    return high, low, twist.astype(np.float32)


def scatter(both_ref, out_ref, wide, tall):
    modes = both_ref.shape[0]
    width = both_ref.shape[1] - LANES
    wide[...] = jnp.zeros_like(wide)
    at = pl.multiple_of(lax.rem(lax.axis_index(PAIR), LANES // modes) * modes, modes)
    wide[pl.ds(at, modes), :] = both_ref[:, :LANES]
    tall[...] = wide[...].T
    half = modes // 2
    rest = width - LANES
    for pair in range(PAIRS):
        for high in range(2):
            rows = tall[pl.ds(8 * high + pair, LANES // FAST, stride=FAST), :]
            out_ref[pair, pl.ds(high * 8, 8), :] = rows
        out_ref[pair, pl.ds(16, modes), :] = both_ref[:, LANES : 2 * LANES]
        for part in range(2):
            to = (pair, pl.ds(16 + modes, half), pl.ds(part * rest, rest))
            out_ref[to] = both_ref[pl.ds(part * half, half), 2 * LANES :]


def spread(got_ref, out_ref):
    for quad in range(PAIRS // 4):
        joined = None
        for sender in range(4 * quad, 4 * quad + 4):
            rows = got_ref[sender, pl.ds(0, 16), :]
            joined = rows if joined is None else joined + rows
        lanes = pl.ds(quad * LANES, LANES)
        out_ref[:, :, lanes] = jnp.broadcast_to(joined, (BLOCKS,) + joined.shape)


def order_modes(own_ref, other_ref, high_ref, low_ref, whole):
    side = lax.axis_index(SIDE)
    modes = MODES // PAIRS
    half = modes // 2
    width = whole.shape[1]
    rest = width - LANES
    for ref, which in ((own_ref, side), (other_ref, 1 - side)):
        for sender in range(PAIRS):
            at = sender * modes
            whole[pl.ds(at, modes), :LANES] = ref[sender, pl.ds(0, modes), :]
            for part in range(2):
                whole[pl.ds(at + part * half, half), LANES:] = ref[
                    sender, pl.ds(modes, half), pl.ds(part * rest, rest)
                ]
        to = (pl.ds(pl.multiple_of(which * width, width), width), slice(None))
        high_ref[to], low_ref[to] = split(whole[...].T)


def index_of(axes, **at):
    index = 0
    for axis in axes:
        index = index * dict(zip(PARTS, SIZES))[axis] + at[axis]
    return index


def places(axes):
    sizes = dict(zip(PARTS, SIZES))
    grid = np.indices([sizes[a] for a in axes]).reshape(len(axes), -1)
    return [dict(zip(axes, map(int, column))) for column in grid.T]


def contract(high_ref, low_ref, steps_ref, out_ref):
    steps = [
        steps_ref[:, pl.ds(8 * high, 8), :].reshape(LANES, MODES) for high in range(2)
    ]
    stress = product(
        (high_ref[...], low_ref[...]), split(jnp.concatenate(steps)), NT
    )
    for side in range(2):
        for share in range(SHARES):
            owner = index_of(LAST, **{SIDE: side}, **places(MODE)[share])
            first = (side * SHARES + share) * OWNED
            for high in range(2):
                out_ref[owner, pl.ds(high * OWNED, OWNED), :] = stress[
                    first : first + OWNED, high * LANES : (high + 1) * LANES
                ]


def plus(a, b):
    return a[0] + b[0], a[1] + b[1]


def minus(a, b):
    return a[0] - b[0], a[1] - b[1]


def by_minus_i(a):
    return a[1], -a[0]


def times(a, real, imag):
    return a[0] * real - a[1] * imag, a[0] * imag + a[1] * real


def transform(values):
    size = len(values)
    if size == 1:
        return values
    even, odd = transform(values[::2]), transform(values[1::2])
    low, high = [], []
    for k in range(size // 2):
        turned = odd[k]
        if 4 * k == size:
            turned = by_minus_i(turned)
        elif k:
            turned = times(
                turned,
                float(np.cos(2 * np.pi * k / size)),
                float(-np.sin(2 * np.pi * k / size)),
            )
        low.append(plus(even[k], turned))
        high.append(minus(even[k], turned))
    return low + high


def spectra(got_ref, high_ref, low_ref, twist_ref, out_ref, rows_high, rows_low, stage):
    for n2 in range(FAST):
        for side in range(2):
            at = (pl.ds(n2 * PADDED, OWNED), pl.ds(side * LANES, LANES))
            rows = pl.ds(n2 // 8 * OWNED, OWNED)
            place = places(PAIR)[n2 % 8]
            senders = [index_of(LAST, **{SIDE: side}, y2=y2, **place) for y2 in range(2)]
            value = got_ref[senders[0], rows, :] + got_ref[senders[1], rows, :]
            rows_high[at], rows_low[at] = split(value)
    stage[...] = product(
        (rows_high[...], rows_low[...]), (high_ref[...], low_ref[...]), NN
    )
    tiles = STEPS // 2 // LANES
    for top in range(0, OWNED, 8):
        for left in range(0, SLOW, LANES):
            values = []
            for n2 in range(FAST):
                rows = pl.ds(n2 * PADDED + top, 8)
                value = (
                    stage[rows, pl.ds(left, LANES)],
                    stage[rows, pl.ds(SLOW + left, LANES)],
                )
                if n2:
                    lanes = pl.ds(left, LANES)
                    value = times(
                        value,
                        twist_ref[0, pl.ds(n2, 1), lanes],
                        twist_ref[1, pl.ds(n2, 1), lanes],
                    )
                values.append(value)
            valid = min(8, OWNED - top)
            for k2, value in enumerate(transform(values)[: FAST // 2]):
                tile = (k2 * SLOW + left) // LANES
                for part in range(2):
                    first = (top * tiles + tile) * 2 + part
                    to = pl.ds(first, valid, stride=2 * tiles)
                    out_ref[to, :] = value[part][:valid]


def call(kernel, shapes, *args, scratch=(), space=pltpu.VMEM, limit=8 << 20):
    whole = pl.BlockSpec(memory_space=pltpu.VMEM)
    return pl.pallas_call(
        kernel,
        out_shape=shapes,
        in_specs=[pl.BlockSpec(memory_space=space)] * len(args),
        out_specs=jax.tree.map(lambda _: whole, shapes),
        scratch_shapes=scratch,
        compiler_params=pltpu.CompilerParams(vmem_limit_bytes=limit),
        cost_estimate=pl.CostEstimate(
            flops=0,
            transcendentals=0,
            bytes_accessed=sum(a.size * a.dtype.itemsize for a in args),
        ),
    )(*args)


def per_device(modal_history, stress_modes):
    modes, width = stress_modes.shape
    shape = jax.ShapeDtypeStruct
    vmem = pltpu.VMEM
    sent = call(
        scatter,
        shape((PAIRS, 16 + 48, LANES), f32),
        jnp.concatenate([modal_history.T, stress_modes], axis=1),
        scratch=[vmem((LANES, LANES), f32)] * 2,
    )
    got = lax.all_to_all(sent, PAIR, split_axis=0, concat_axis=0, tiled=True)
    history = call(spread, shape((BLOCKS, 16, MODES), f32), got)
    steps = lax.all_to_all(history, PLANE, split_axis=0, concat_axis=0, tiled=True)
    own = got[:, 16:]
    high, low = call(
        order_modes,
        (shape((2 * width, MODES), bf16), shape((2 * width, MODES), bf16)),
        own,
        lax.ppermute(own, SIDE, [(0, 1), (1, 0)]),
        scratch=[vmem((MODES, width), f32)],
    )
    stress = call(
        contract,
        shape((2 * SHARES, 2 * OWNED, LANES), f32),
        high,
        low,
        steps,
    )
    owned = lax.all_to_all(stress, LAST, split_axis=0, concat_axis=0, tiled=True)
    first_high, first_low, twist = tables()
    rows = FAST * PADDED
    out = call(
        spectra,
        shape((OWNED * STEPS // LANES, LANES), f32),
        owned,
        first_high,
        first_low,
        twist,
        scratch=[vmem((rows, SLOW), bf16)] * 2 + [vmem((rows, 2 * SLOW), f32)],
    )
    out = out.reshape(OWNED, STEPS // 2 // LANES, 2, LANES).transpose(0, 2, 1, 3)
    return out.reshape(OWNED, 2, STEPS // 2)


def solution(mesh):
    parts = Mesh(mesh.devices.reshape(SIZES), PARTS)
    return jax.shard_map(
        per_device,
        mesh=parts,
        in_specs=(P(ELEM, MODE), P(MODE, ELEM)),
        out_specs=P(PARTS, None, None),
        check_vma=False,
    )
```

```python
import numpy as np

import jax
import jax.numpy as jnp
from jax import lax
from jax.experimental import pallas as pl
from jax.experimental.pallas import tpu as pltpu
from jax.sharding import Mesh, PartitionSpec as P

PARTS = ("z2", "z1", "z0", "y1", "y0", "x1", "x0", "y2", "c")
SIZES = (2,) * 9
ELEM = ("z2", "z1", "z0", "y1", "y0")
MODE = ("x1", "x0", "y2", "c")
PAIR = ("x1", "x0", "c")
PLANE = ("y1", "z2", "z1", "z0")
SIDE = "y0"
LAST = ("y2", "y0", "c", "x1", "x0")
BLOCKS, SHARES, PAIRS = 16, 16, 8
STEPS, MODES = 4096, 256
SLOW, FAST = 256, 16
OWNED, PADDED = 12, 16
LANES = 128
f32, bf16 = jnp.float32, jnp.bfloat16
NN = (((1,), (0,)), ((), ()))
NT = (((1,), (1,)), ((), ()))


def split(x):
    high = x.astype(bf16)
    return high, (x - high.astype(f32)).astype(bf16)


def product(a, b, dims):
    (ah, al), (bh, bl) = a, b
    dot = lambda x, y: lax.dot_general(x, y, dims, preferred_element_type=f32)
    return dot(ah, bh) + (dot(ah, bl) + dot(al, bh))


def tables():
    k1 = np.arange(SLOW)
    angle = 2.0 * np.pi * ((k1[:, None] * k1[None, :]) % SLOW) / SLOW
    first = np.concatenate([np.cos(angle), -np.sin(angle)], axis=1) / np.sqrt(STEPS)
    first = first.reshape(2 * BLOCKS, 8, 2 * SLOW)
    order = [
        index_of(ELEM, **{SIDE: side}, **place) for side in range(2) for place in places(PLANE)
    ]
    first = first[np.array(order)].reshape(SLOW, 2 * SLOW)
    high = first.astype(np.float32).astype(jnp.bfloat16)
    low = (first - high.astype(np.float64)).astype(jnp.bfloat16)
    turn = 2.0 * np.pi * (np.arange(FAST)[:, None] * k1[None, :]) / STEPS
    twist = np.stack([np.cos(turn), -np.sin(turn)])
    return high, low, twist.astype(np.float32)


def scatter(both_ref, out_ref, wide, tall):
    modes = both_ref.shape[0]
    width = both_ref.shape[1] - LANES
    wide[...] = jnp.zeros_like(wide)
    wide[pl.ds(0, modes), :] = both_ref[:, :LANES]
    tall[...] = wide[...].T
    turn = lax.rem(lax.axis_index(PAIR), 4)
    half = modes // 2
    rest = width - LANES
    turns = [lax.rem(quarter + turn, 4) * modes for quarter in range(4)]
    for pair in range(PAIRS):
        first = pair % 2 * half
        out_ref[pair, pl.ds(0, half), :] = both_ref[pl.ds(first, half), LANES : 2 * LANES]
        for part in range(2):
            to = (pair, pl.ds(half, half // 2), pl.ds(part * rest, rest))
            from_rows = pl.ds(first + part * (half // 2), half // 2)
            out_ref[to] = both_ref[from_rows, 2 * LANES :]
        joined = None
        for quarter in range(4):
            first = 8 * (quarter // 2) + pair + 4 * (quarter % 2) * FAST
            rows = tall[pl.ds(first, 4, stride=FAST), :]
            rows = pltpu.roll(rows, turns[quarter], 1)
            joined = rows if joined is None else joined + rows
        out_ref[pair, pl.ds(modes * 3 // 4, 4), :] = joined


def spread(got_ref, out_ref):
    lane = lax.broadcasted_iota(jnp.int32, (4, LANES), 1) // (LANES // 4)
    for quad in range(PAIRS // 4):
        senders = [got_ref[4 * quad + k, pl.ds(24, 4), :] for k in range(4)]
        quarters = []
        for quarter in range(4):
            value = senders[-quarter % 4]
            for k in range(1, 4):
                value = jnp.where(lane == k, senders[(k - quarter) % 4], value)
            if quarter:
                value = pltpu.roll(value, LANES - quarter * LANES // 4, 1)
            quarters.append(value)
        joined = jnp.concatenate(quarters)
        lanes = pl.ds(quad * LANES, LANES)
        out_ref[:, :, lanes] = jnp.broadcast_to(joined, (BLOCKS,) + joined.shape)


def order_modes(own_ref, core_ref, side_ref, both_ref, high_ref, low_ref, whole):
    side, core = lax.axis_index(SIDE), lax.axis_index("c")
    modes = MODES // PAIRS
    half = modes // 2
    width = whole.shape[1]
    rest = width - LANES
    for refs, which in (
        ((own_ref, core_ref), side),
        ((side_ref, both_ref), 1 - side),
    ):
        for ref, upper in zip(refs, (core, 1 - core)):
            for sender in range(PAIRS):
                at = pl.multiple_of(sender * modes + upper * half, half)
                whole[pl.ds(at, half), :LANES] = ref[sender, pl.ds(0, half), :]
                for part in range(2):
                    rows = pl.ds(pl.multiple_of(at + part * (half // 2), 8), half // 2)
                    whole[rows, LANES:] = ref[
                        sender, pl.ds(half, half // 2), pl.ds(part * rest, rest)
                    ]
        to = (pl.ds(pl.multiple_of(which * width, width), width), slice(None))
        high_ref[to], low_ref[to] = split(whole[...].T)


def index_of(axes, **at):
    index = 0
    for axis in axes:
        index = index * dict(zip(PARTS, SIZES))[axis] + at[axis]
    return index


def places(axes):
    sizes = dict(zip(PARTS, SIZES))
    grid = np.indices([sizes[a] for a in axes]).reshape(len(axes), -1)
    return [dict(zip(axes, map(int, column))) for column in grid.T]


def contract(high_ref, low_ref, steps_ref, out_ref):
    steps = [
        steps_ref[:, pl.ds(8 * high, 8), :].reshape(LANES, MODES) for high in range(2)
    ]
    stress = product(
        (high_ref[...], low_ref[...]), split(jnp.concatenate(steps)), NT
    )
    for side in range(2):
        for share in range(SHARES):
            owner = index_of(LAST, **{SIDE: side}, **places(MODE)[share])
            first = (side * SHARES + share) * OWNED
            for high in range(2):
                out_ref[owner, pl.ds(high * OWNED, OWNED), :] = stress[
                    first : first + OWNED, high * LANES : (high + 1) * LANES
                ]


def plus(a, b):
    return a[0] + b[0], a[1] + b[1]


def minus(a, b):
    return a[0] - b[0], a[1] - b[1]


def by_minus_i(a):
    return a[1], -a[0]


def times(a, real, imag):
    return a[0] * real - a[1] * imag, a[0] * imag + a[1] * real


def transform(values):
    size = len(values)
    if size == 1:
        return values
    even, odd = transform(values[::2]), transform(values[1::2])
    low, high = [], []
    for k in range(size // 2):
        turned = odd[k]
        if 4 * k == size:
            turned = by_minus_i(turned)
        elif k:
            turned = times(
                turned,
                float(np.cos(2 * np.pi * k / size)),
                float(-np.sin(2 * np.pi * k / size)),
            )
        low.append(plus(even[k], turned))
        high.append(minus(even[k], turned))
    return low + high


def spectra(got_ref, high_ref, low_ref, twist_ref, out_ref, rows_high, rows_low, stage):
    for n2 in range(FAST):
        for side in range(2):
            at = (pl.ds(n2 * PADDED, OWNED), pl.ds(side * LANES, LANES))
            rows = pl.ds(n2 // 8 * OWNED, OWNED)
            place = places(PAIR)[n2 % 8]
            senders = [index_of(LAST, **{SIDE: side}, y2=y2, **place) for y2 in range(2)]
            value = got_ref[senders[0], rows, :] + got_ref[senders[1], rows, :]
            rows_high[at], rows_low[at] = split(value)
    stage[...] = product(
        (rows_high[...], rows_low[...]), (high_ref[...], low_ref[...]), NN
    )
    tiles = STEPS // 2 // LANES
    for top in range(0, OWNED, 8):
        for left in range(0, SLOW, LANES):
            values = []
            for n2 in range(FAST):
                rows = pl.ds(n2 * PADDED + top, 8)
                value = (
                    stage[rows, pl.ds(left, LANES)],
                    stage[rows, pl.ds(SLOW + left, LANES)],
                )
                if n2:
                    lanes = pl.ds(left, LANES)
                    value = times(
                        value,
                        twist_ref[0, pl.ds(n2, 1), lanes],
                        twist_ref[1, pl.ds(n2, 1), lanes],
                    )
                values.append(value)
            valid = min(8, OWNED - top)
            for k2, value in enumerate(transform(values)[: FAST // 2]):
                tile = (k2 * SLOW + left) // LANES
                for part in range(2):
                    first = (top * tiles + tile) * 2 + part
                    to = pl.ds(first, valid, stride=2 * tiles)
                    out_ref[to, :] = value[part][:valid]


def call(kernel, shapes, *args, scratch=(), space=pltpu.VMEM, limit=8 << 20):
    whole = pl.BlockSpec(memory_space=pltpu.VMEM)
    return pl.pallas_call(
        kernel,
        out_shape=shapes,
        in_specs=[pl.BlockSpec(memory_space=space)] * len(args),
        out_specs=jax.tree.map(lambda _: whole, shapes),
        scratch_shapes=scratch,
        compiler_params=pltpu.CompilerParams(vmem_limit_bytes=limit),
        cost_estimate=pl.CostEstimate(
            flops=0,
            transcendentals=0,
            bytes_accessed=sum(a.size * a.dtype.itemsize for a in args),
        ),
    )(*args)


def per_device(modal_history, stress_modes):
    modes, width = stress_modes.shape
    shape = jax.ShapeDtypeStruct
    vmem = pltpu.VMEM
    sent = call(
        scatter,
        shape((PAIRS, 24 + 4, LANES), f32),
        jnp.concatenate([modal_history.T, stress_modes], axis=1),
        scratch=[vmem((LANES, LANES), f32)] * 2,
    )
    got = lax.all_to_all(sent, PAIR, split_axis=0, concat_axis=0, tiled=True)
    history = call(spread, shape((BLOCKS, 16, MODES), f32), got)
    steps = lax.all_to_all(history, PLANE, split_axis=0, concat_axis=0, tiled=True)
    own = got[:, :24]
    core = lax.ppermute(own, "c", [(0, 1), (1, 0)])
    side = lax.ppermute(own, SIDE, [(0, 1), (1, 0)])
    both = lax.ppermute(own, (SIDE, "c"), [(i, i ^ 3) for i in range(4)])
    high, low = call(
        order_modes,
        (shape((2 * width, MODES), bf16), shape((2 * width, MODES), bf16)),
        own,
        core,
        side,
        both,
        scratch=[vmem((MODES, width), f32)],
    )
    stress = call(
        contract,
        shape((2 * SHARES, 2 * OWNED, LANES), f32),
        high,
        low,
        steps,
    )
    owned = lax.all_to_all(stress, LAST, split_axis=0, concat_axis=0, tiled=True)
    first_high, first_low, twist = tables()
    rows = FAST * PADDED
    out = call(
        spectra,
        shape((OWNED * STEPS // LANES, LANES), f32),
        owned,
        first_high,
        first_low,
        twist,
        scratch=[vmem((rows, SLOW), bf16)] * 2 + [vmem((rows, 2 * SLOW), f32)],
    )
    out = out.reshape(OWNED, STEPS // 2 // LANES, 2, LANES).transpose(0, 2, 1, 3)
    return out.reshape(OWNED, 2, STEPS // 2)


def solution(mesh):
    parts = Mesh(mesh.devices.reshape(SIZES), PARTS)
    return jax.shard_map(
        per_device,
        mesh=parts,
        in_specs=(P(ELEM, MODE), P(MODE, ELEM)),
        out_specs=P(PARTS, None, None),
        check_vma=False,
    )
```

```python
import numpy as np

import jax
import jax.numpy as jnp
from jax import lax
from jax.experimental import pallas as pl
from jax.experimental.pallas import tpu as pltpu
from jax.sharding import Mesh, PartitionSpec as P

PARTS = ("z2", "z1", "z0", "y1", "y0", "x1", "x0", "y2", "c")
SIZES = (2,) * 9
ELEM = ("z2", "z1", "z0", "y1", "y0")
MODE = ("x1", "x0", "y2", "c")
PAIR = ("x1", "x0", "c")
PLANE = ("y1", "z2", "z1", "z0")
SIDE = "y0"
LAST = ("y2", "c", "y0", "x1", "x0")
BLOCKS, SHARES, PAIRS = 16, 16, 8
STEPS, MODES = 4096, 256
SLOW, FAST = 256, 16
OWNED = 12
LANES = 128
f32, bf16 = jnp.float32, jnp.bfloat16
NN = (((1,), (0,)), ((), ()))
NT = (((1,), (1,)), ((), ()))


def split(x):
    high = x.astype(bf16)
    return high, (x - high.astype(f32)).astype(bf16)


def product(a, b, dims):
    return lax.dot_general(a, b, dims, preferred_element_type=f32)


def tables():
    k1 = np.arange(SLOW)
    angle = 2.0 * np.pi * ((k1[:, None] * k1[None, :]) % SLOW) / SLOW
    first = np.concatenate([np.cos(angle), -np.sin(angle)], axis=1) / np.sqrt(STEPS)
    first = first.reshape(2 * BLOCKS, 8, 2 * SLOW)
    order = [
        index_of(ELEM, **{SIDE: side}, **place) for side in range(2) for place in places(PLANE)
    ]
    first = first[np.array(order)].reshape(SLOW, 2 * SLOW)
    high = first.astype(np.float32).astype(jnp.bfloat16)
    low = (first - high.astype(np.float64)).astype(jnp.bfloat16)
    turn = 2.0 * np.pi * (np.arange(FAST)[:, None] * k1[None, :]) / STEPS
    twist = np.stack([np.cos(turn), -np.sin(turn)])
    return np.concatenate([high, low, high]), twist.astype(np.float32)


def scatter(both_ref, out_ref, wide, tall):
    modes = both_ref.shape[0]
    width = both_ref.shape[1] - LANES
    wide[...] = jnp.zeros_like(wide)
    wide[pl.ds(0, modes), :] = both_ref[:, :LANES]
    tall[...] = wide[...].T
    turn = lax.rem(lax.axis_index(PAIR), 4)
    half = modes // 2
    rest = width - LANES
    turns = [lax.rem(quarter + turn, 4) * modes for quarter in range(4)]
    for pair in range(PAIRS):
        first = pair % 2 * half
        out_ref[pair, pl.ds(0, half), :] = both_ref[pl.ds(first, half), LANES : 2 * LANES]
        for part in range(2):
            to = (pair, pl.ds(half, half // 2), pl.ds(part * rest, rest))
            from_rows = pl.ds(first + part * (half // 2), half // 2)
            out_ref[to] = both_ref[from_rows, 2 * LANES :]
        joined = None
        for quarter in range(4):
            first = 8 * (quarter // 2) + pair + 4 * (quarter % 2) * FAST
            rows = tall[pl.ds(first, 4, stride=FAST), :]
            rows = pltpu.roll(rows, turns[quarter], 1)
            joined = rows if joined is None else joined + rows
        out_ref[pair, pl.ds(modes * 3 // 4, 4), :] = joined


def spread(got_ref, out_ref):
    lane = lax.broadcasted_iota(jnp.int32, (4, LANES), 1) // (LANES // 4)
    for quad in range(PAIRS // 4):
        senders = [got_ref[4 * quad + k, pl.ds(24, 4), :] for k in range(4)]
        quarters = []
        for quarter in range(4):
            value = senders[-quarter % 4]
            for k in range(1, 4):
                value = jnp.where(lane == k, senders[(k - quarter) % 4], value)
            if quarter:
                value = pltpu.roll(value, LANES - quarter * LANES // 4, 1)
            quarters.append(value)
        joined = jnp.concatenate(quarters)
        lanes = pl.ds(quad * LANES, LANES)
        out_ref[:, :, lanes] = jnp.broadcast_to(joined, (BLOCKS,) + joined.shape)


def order_modes(own_ref, core_ref, side_ref, both_ref, out_ref, whole):
    side, core = lax.axis_index(SIDE), lax.axis_index("c")
    modes = MODES // PAIRS
    half = modes // 2
    width = whole.shape[1]
    rest = width - LANES
    for refs, which in (
        ((own_ref, core_ref), side),
        ((side_ref, both_ref), 1 - side),
    ):
        for ref, upper in zip(refs, (core, 1 - core)):
            for sender in range(PAIRS):
                at = pl.multiple_of(sender * modes + upper * half, half)
                whole[pl.ds(at, half), :LANES] = ref[sender, pl.ds(0, half), :]
                for part in range(2):
                    rows = pl.ds(pl.multiple_of(at + part * (half // 2), 8), half // 2)
                    whole[rows, LANES:] = ref[
                        sender, pl.ds(half, half // 2), pl.ds(part * rest, rest)
                    ]
        to = pl.ds(pl.multiple_of(which * width, width), width)
        high, low = split(whole[...].T)
        for part, value in enumerate((high, high, low)):
            out_ref[to, pl.ds(part * MODES, MODES)] = value


def index_of(axes, **at):
    index = 0
    for axis in axes:
        index = index * dict(zip(PARTS, SIZES))[axis] + at[axis]
    return index


def places(axes):
    sizes = dict(zip(PARTS, SIZES))
    grid = np.indices([sizes[a] for a in axes]).reshape(len(axes), -1)
    return [dict(zip(axes, map(int, column))) for column in grid.T]


def contract(modes_ref, steps_ref, out_ref):
    steps = [
        steps_ref[:, pl.ds(8 * high, 8), :].reshape(LANES, MODES) for high in range(2)
    ]
    high, low = split(jnp.concatenate(steps))
    parts = jnp.concatenate([high, low, high], axis=1)
    stress = product(modes_ref[...], parts, NT)
    for side in range(2):
        for share in range(SHARES):
            owner = index_of(LAST, **{SIDE: side}, **places(MODE)[share])
            first = (side * SHARES + share) * OWNED
            for high in range(2):
                out_ref[owner, pl.ds(high * OWNED, OWNED), :] = stress[
                    first : first + OWNED, high * LANES : (high + 1) * LANES
                ]


def plus(a, b):
    return a[0] + b[0], a[1] + b[1]


def minus(a, b):
    return a[0] - b[0], a[1] - b[1]


def by_minus_i(a):
    return a[1], -a[0]


def times(a, real, imag):
    return a[0] * real - a[1] * imag, a[0] * imag + a[1] * real


def transform(values):
    size = len(values)
    if size == 1:
        return values
    even, odd = transform(values[::2]), transform(values[1::2])
    low, high = [], []
    for k in range(size // 2):
        turned = odd[k]
        if 4 * k == size:
            turned = by_minus_i(turned)
        elif k:
            turned = times(
                turned,
                float(np.cos(2 * np.pi * k / size)),
                float(-np.sin(2 * np.pi * k / size)),
            )
        low.append(plus(even[k], turned))
        high.append(minus(even[k], turned))
    return low + high


def spectra(got_ref, first_ref, twist_ref, out_hbm, rows, stage, result, sems):
    tops = ((0, 8, 0), (8, OWNED - 8, 8 * FAST))
    for n2 in range(FAST):
        for side in range(2):
            part = pl.ds(n2 // 8 * OWNED, OWNED)
            place = places(PAIR)[n2 % 8]
            senders = [index_of(LAST, **{SIDE: side}, y2=y2, **place) for y2 in range(2)]
            value = got_ref[senders[0], part, :] + got_ref[senders[1], part, :]
            for top, count, base in tops:
                at = (pl.ds(base + n2 * count, count), pl.ds(side * LANES, LANES))
                rows[at] = value[top : top + count]
    high, low = split(rows[...])
    parts = jnp.concatenate([high, high, low], axis=1)
    stage[...] = product(parts, first_ref[...], NN)
    tiles = STEPS // 2 // LANES
    copies = []
    for top, count, base in tops:
        for left in range(0, SLOW, LANES):
            values = []
            for n2 in range(FAST):
                at = pl.ds(base + n2 * count, count)
                value = (
                    stage[at, pl.ds(left, LANES)],
                    stage[at, pl.ds(SLOW + left, LANES)],
                )
                if n2:
                    lanes = pl.ds(left, LANES)
                    value = times(
                        value,
                        twist_ref[0, pl.ds(n2, 1), lanes],
                        twist_ref[1, pl.ds(n2, 1), lanes],
                    )
                values.append(value)
            for k2, value in enumerate(transform(values)[: FAST // 2]):
                tile = (k2 * SLOW + left) // LANES
                for part in range(2):
                    first = (top * tiles + tile) * 2 + part
                    result[pl.ds(first, count, stride=2 * tiles), :] = value[part]
        done = pl.ds(top * 2 * tiles, count * 2 * tiles)
        copy = pltpu.make_async_copy(
            result.at[done, :], out_hbm.at[done, :], sems.at[len(copies)]
        )
        copy.start()
        copies.append(copy)
    for copy in copies:
        copy.wait()


def call(kernel, shapes, *args, scratch=(), space=pltpu.VMEM, out=pltpu.VMEM, limit=8 << 20):
    whole = pl.BlockSpec(memory_space=out)
    return pl.pallas_call(
        kernel,
        out_shape=shapes,
        in_specs=[pl.BlockSpec(memory_space=space)] * len(args),
        out_specs=jax.tree.map(lambda _: whole, shapes),
        scratch_shapes=scratch,
        compiler_params=pltpu.CompilerParams(vmem_limit_bytes=limit),
        cost_estimate=pl.CostEstimate(
            flops=0,
            transcendentals=0,
            bytes_accessed=sum(a.size * a.dtype.itemsize for a in args),
        ),
    )(*args)


def per_device(modal_history, stress_modes):
    modes, width = stress_modes.shape
    shape = jax.ShapeDtypeStruct
    vmem = pltpu.VMEM
    sent = call(
        scatter,
        shape((PAIRS, 24 + 4, LANES), f32),
        jnp.concatenate([modal_history.T, stress_modes], axis=1),
        scratch=[vmem((LANES, LANES), f32)] * 2,
    )
    got = lax.all_to_all(sent, PAIR, split_axis=0, concat_axis=0, tiled=True)
    history = call(spread, shape((BLOCKS, 16, MODES), f32), got)
    steps = lax.all_to_all(history, PLANE, split_axis=0, concat_axis=0, tiled=True)
    own = got[:, :24]
    core = lax.ppermute(own, "c", [(0, 1), (1, 0)])
    side = lax.ppermute(own, SIDE, [(0, 1), (1, 0)])
    both = lax.ppermute(own, (SIDE, "c"), [(i, i ^ 3) for i in range(4)])
    ordered = call(
        order_modes,
        shape((2 * width, 3 * MODES), bf16),
        own,
        core,
        side,
        both,
        scratch=[vmem((MODES, width), f32)],
    )
    stress = call(
        contract,
        shape((2 * SHARES, 2 * OWNED, LANES), f32),
        ordered,
        steps,
    )
    owned = lax.all_to_all(stress, LAST, split_axis=0, concat_axis=0, tiled=True)
    first, twist = tables()
    rows = FAST * OWNED
    out = call(
        spectra,
        shape((OWNED * STEPS // LANES, LANES), f32),
        owned,
        first,
        twist,
        scratch=[vmem((rows, SLOW), f32), vmem((rows, 2 * SLOW), f32)]
        + [vmem((OWNED * STEPS // LANES, LANES), f32), pltpu.SemaphoreType.DMA((2,))],
        out=pltpu.HBM,
    )
    out = out.reshape(OWNED, STEPS // 2 // LANES, 2, LANES).transpose(0, 2, 1, 3)
    return out.reshape(OWNED, 2, STEPS // 2)


def solution(mesh):
    parts = Mesh(mesh.devices.reshape(SIZES), PARTS)
    return jax.shard_map(
        per_device,
        mesh=parts,
        in_specs=(P(ELEM, MODE), P(MODE, ELEM)),
        out_specs=P(PARTS, None, None),
        check_vma=False,
    )
```

```python
import numpy as np

import jax
import jax.numpy as jnp
from jax import lax
from jax.experimental import pallas as pl
from jax.experimental.pallas import tpu as pltpu
from jax.sharding import Mesh, PartitionSpec as P

PARTS = ("z2", "z1", "z0", "y1", "y0", "x1", "x0", "y2", "c")
SIZES = (2,) * 9
ELEM = ("z2", "z1", "z0", "y1", "y0")
MODE = ("x1", "x0", "y2", "c")
PAIR = ("x1", "x0", "c")
PLANE = ("y1", "z2", "z1", "z0")
SIDE = "y0"
LAST = ("y2", "c", "y0", "x1", "x0")
BLOCKS, SHARES, PAIRS = 16, 16, 8
STEPS, MODES = 4096, 256
SLOW, FAST = 256, 16
OWNED = 12
LANES = 128
f32, bf16 = jnp.float32, jnp.bfloat16
NN = (((1,), (0,)), ((), ()))
NT = (((1,), (1,)), ((), ()))


def split(x):
    high = x.astype(bf16)
    return high, (x - high.astype(f32)).astype(bf16)


def product(a, b, dims):
    return lax.dot_general(a, b, dims, preferred_element_type=f32)


def tables():
    k1 = np.arange(SLOW)
    angle = 2.0 * np.pi * ((k1[:, None] * k1[None, :]) % SLOW) / SLOW
    first = np.concatenate([np.cos(angle), -np.sin(angle)], axis=1) / np.sqrt(STEPS)
    first = first.reshape(2 * BLOCKS, 8, 2 * SLOW)
    order = [
        index_of(ELEM, **{SIDE: side}, **place) for side in range(2) for place in places(PLANE)
    ]
    first = first[np.array(order)].reshape(SLOW, 2 * SLOW)
    high = first.astype(np.float32).astype(jnp.bfloat16)
    low = (first - high.astype(np.float64)).astype(jnp.bfloat16)
    turn = 2.0 * np.pi * (np.arange(FAST)[:, None] * k1[None, :]) / STEPS
    twist = np.stack([np.cos(turn), -np.sin(turn)])
    return np.concatenate([high, low, high]), twist.astype(np.float32)


def scatter(both_ref, out_ref, wide, tall):
    modes = both_ref.shape[0]
    width = both_ref.shape[1] - LANES
    wide[...] = jnp.zeros_like(wide)
    wide[pl.ds(0, modes), :] = both_ref[:, :LANES]
    tall[...] = wide[...].T
    turn = lax.rem(lax.axis_index(PAIR), 4)
    half = modes // 2
    rest = width - LANES
    turns = [lax.rem(quarter + turn, 4) * modes for quarter in range(4)]
    for pair in range(PAIRS):
        first = pair % 2 * half
        out_ref[pair, pl.ds(0, half), :] = both_ref[pl.ds(first, half), LANES : 2 * LANES]
        for part in range(2):
            to = (pair, pl.ds(half, half // 2), pl.ds(part * rest, rest))
            from_rows = pl.ds(first + part * (half // 2), half // 2)
            out_ref[to] = both_ref[from_rows, 2 * LANES :]
        joined = None
        for quarter in range(4):
            first = 8 * (quarter // 2) + pair + 4 * (quarter % 2) * FAST
            rows = tall[pl.ds(first, 4, stride=FAST), :]
            rows = pltpu.roll(rows, turns[quarter], 1)
            joined = rows if joined is None else joined + rows
        out_ref[pair, pl.ds(modes * 3 // 4, 4), :] = joined


def spread(got_ref, out_ref):
    lane = lax.broadcasted_iota(jnp.int32, (4, LANES), 1) // (LANES // 4)
    for quad in range(PAIRS // 4):
        senders = [got_ref[4 * quad + k, pl.ds(24, 4), :] for k in range(4)]
        quarters = []
        for quarter in range(4):
            value = senders[-quarter % 4]
            for k in range(1, 4):
                value = jnp.where(lane == k, senders[(k - quarter) % 4], value)
            if quarter:
                value = pltpu.roll(value, LANES - quarter * LANES // 4, 1)
            quarters.append(value)
        joined = jnp.concatenate(quarters)
        lanes = pl.ds(quad * LANES, LANES)
        out_ref[:, :, lanes] = jnp.broadcast_to(joined, (BLOCKS,) + joined.shape)


def order_modes(own_ref, core_ref, side_ref, both_ref, out_ref, whole):
    side, core = lax.axis_index(SIDE), lax.axis_index("c")
    modes = MODES // PAIRS
    half = modes // 2
    width = whole.shape[1]
    rest = width - LANES
    for refs, which in (
        ((own_ref, core_ref), side),
        ((side_ref, both_ref), 1 - side),
    ):
        for ref, upper in zip(refs, (core, 1 - core)):
            for sender in range(PAIRS):
                at = pl.multiple_of(sender * modes + upper * half, half)
                whole[pl.ds(at, half), :LANES] = ref[sender, pl.ds(0, half), :]
                for part in range(2):
                    rows = pl.ds(pl.multiple_of(at + part * (half // 2), 8), half // 2)
                    whole[rows, LANES:] = ref[
                        sender, pl.ds(half, half // 2), pl.ds(part * rest, rest)
                    ]
        to = pl.ds(pl.multiple_of(which * width, width), width)
        high, low = split(whole[...].T)
        for part, value in enumerate((high, high, low)):
            out_ref[to, pl.ds(part * MODES, MODES)] = value


def index_of(axes, **at):
    index = 0
    for axis in axes:
        index = index * dict(zip(PARTS, SIZES))[axis] + at[axis]
    return index


def places(axes):
    sizes = dict(zip(PARTS, SIZES))
    grid = np.indices([sizes[a] for a in axes]).reshape(len(axes), -1)
    return [dict(zip(axes, map(int, column))) for column in grid.T]


def contract(modes_ref, steps_ref, out_ref):
    steps = [
        steps_ref[:, pl.ds(8 * high, 8), :].reshape(LANES, MODES) for high in range(2)
    ]
    high, low = split(jnp.concatenate(steps))
    parts = jnp.concatenate([high, low, high], axis=1)
    stress = product(modes_ref[...], parts, NT)
    for side in range(2):
        for share in range(SHARES):
            owner = index_of(LAST, **{SIDE: side}, **places(MODE)[share])
            first = (side * SHARES + share) * OWNED
            for high in range(2):
                out_ref[owner, pl.ds(high * OWNED, OWNED), :] = stress[
                    first : first + OWNED, high * LANES : (high + 1) * LANES
                ]


def plus(a, b):
    return a[0] + b[0], a[1] + b[1]


def minus(a, b):
    return a[0] - b[0], a[1] - b[1]


def by_minus_i(a):
    return a[1], -a[0]


def times(a, real, imag):
    return a[0] * real - a[1] * imag, a[0] * imag + a[1] * real


def transform(values):
    size = len(values)
    if size == 1:
        return values
    even, odd = transform(values[::2]), transform(values[1::2])
    low, high = [], []
    for k in range(size // 2):
        turned = odd[k]
        if 4 * k == size:
            turned = by_minus_i(turned)
        elif k:
            turned = times(
                turned,
                float(np.cos(2 * np.pi * k / size)),
                float(-np.sin(2 * np.pi * k / size)),
            )
        low.append(plus(even[k], turned))
        high.append(minus(even[k], turned))
    return low + high


def spectra(got_ref, first_ref, twist_ref, out_hbm, rows, stage, result, sems):
    tops = ((0, 8, 0), (8, OWNED - 8, 8 * FAST))
    for n2 in range(FAST):
        for side in range(2):
            part = pl.ds(n2 // 8 * OWNED, OWNED)
            place = places(PAIR)[n2 % 8]
            senders = [index_of(LAST, **{SIDE: side}, y2=y2, **place) for y2 in range(2)]
            value = got_ref[senders[0], part, :] + got_ref[senders[1], part, :]
            for top, count, base in tops:
                at = (pl.ds(base + n2 * count, count), pl.ds(side * LANES, LANES))
                rows[at] = value[top : top + count]
    high, low = split(rows[...])
    parts = jnp.concatenate([high, high, low], axis=1)
    stage[...] = product(parts, first_ref[...], NN)
    tiles = STEPS // 2 // LANES
    copies = []
    for top, count, base in tops:
        for left in range(0, SLOW, LANES):
            values = []
            for n2 in range(FAST):
                at = pl.ds(base + n2 * count, count)
                value = (
                    stage[at, pl.ds(left, LANES)],
                    stage[at, pl.ds(SLOW + left, LANES)],
                )
                if n2:
                    lanes = pl.ds(left, LANES)
                    value = times(
                        value,
                        twist_ref[0, pl.ds(n2, 1), lanes],
                        twist_ref[1, pl.ds(n2, 1), lanes],
                    )
                values.append(value)
            for k2, value in enumerate(transform(values)[: FAST // 2]):
                tile = (k2 * SLOW + left) // LANES
                for part in range(2):
                    first = (top * tiles + tile) * 2 + part
                    result[pl.ds(first, count, stride=2 * tiles), :] = value[part]
        done = pl.ds(top * 2 * tiles, count * 2 * tiles)
        copy = pltpu.make_async_copy(
            result.at[done, :], out_hbm.at[done, :], sems.at[len(copies)]
        )
        copy.start()
        copies.append(copy)
    for copy in copies:
        copy.wait()


def call(kernel, shapes, *args, scratch=(), space=pltpu.VMEM, out=pltpu.VMEM, limit=8 << 20):
    whole = pl.BlockSpec(memory_space=out)
    return pl.pallas_call(
        kernel,
        out_shape=shapes,
        in_specs=[pl.BlockSpec(memory_space=space)] * len(args),
        out_specs=jax.tree.map(lambda _: whole, shapes),
        scratch_shapes=scratch,
        compiler_params=pltpu.CompilerParams(vmem_limit_bytes=limit),
        cost_estimate=pl.CostEstimate(
            flops=0,
            transcendentals=0,
            bytes_accessed=sum(a.size * a.dtype.itemsize for a in args),
        ),
    )(*args)


def per_device(modal_history, stress_modes):
    modes, width = stress_modes.shape
    shape = jax.ShapeDtypeStruct
    vmem = pltpu.VMEM
    sent = call(
        scatter,
        shape((PAIRS, 24 + 4, LANES), f32),
        jnp.concatenate([modal_history.T, stress_modes], axis=1),
        scratch=[vmem((LANES, LANES), f32)] * 2,
    )
    got = lax.all_to_all(sent, PAIR, split_axis=0, concat_axis=0, tiled=True)
    history = call(spread, shape((BLOCKS, 16, MODES), f32), got)
    steps = lax.all_to_all(history, PLANE, split_axis=0, concat_axis=0, tiled=True)
    own = got[:, :24]
    core = lax.ppermute(own, "c", [(0, 1), (1, 0)])
    both = lax.ppermute(own, (SIDE, "c"), [(i, i ^ 3) for i in range(4)])
    side = lax.ppermute(own, SIDE, [(0, 1), (1, 0)])
    ordered = call(
        order_modes,
        shape((2 * width, 3 * MODES), bf16),
        own,
        core,
        side,
        both,
        scratch=[vmem((MODES, width), f32)],
    )
    stress = call(
        contract,
        shape((2 * SHARES, 2 * OWNED, LANES), f32),
        ordered,
        steps,
    )
    owned = lax.all_to_all(stress, LAST, split_axis=0, concat_axis=0, tiled=True)
    first, twist = tables()
    rows = FAST * OWNED
    out = call(
        spectra,
        shape((OWNED * STEPS // LANES, LANES), f32),
        owned,
        first,
        twist,
        scratch=[vmem((rows, SLOW), f32), vmem((rows, 2 * SLOW), f32)]
        + [vmem((OWNED * STEPS // LANES, LANES), f32), pltpu.SemaphoreType.DMA((2,))],
        out=pltpu.HBM,
    )
    out = out.reshape(OWNED, STEPS // 2 // LANES, 2, LANES).transpose(0, 2, 1, 3)
    return out.reshape(OWNED, 2, STEPS // 2)


def solution(mesh):
    parts = Mesh(mesh.devices.reshape(SIZES), PARTS)
    return jax.shard_map(
        per_device,
        mesh=parts,
        in_specs=(P(ELEM, MODE), P(MODE, ELEM)),
        out_specs=P(PARTS, None, None),
        check_vma=False,
    )
```
